32 devices in a mesh: row: 8 (over z, x), col: 4 (over y, core).
Axes of the slice: x: 2, y: 2, z: 4, core: 2. Of those that a mesh axis runs over, the one named last changes fastest.
Arguments:
- alignment: bfloat16 [256, 192, 256], P('row', 'col'), may hold values from -8 to 8
- alignment_mask: int32 [256, 192], P('row', 'col'), may hold values from 0 to 1, as said below
- residue_mask: int32 [192], replicated, may hold values from 0 to 1, as said below
- pair_features: bfloat16 [192, 192, 128], P('row', 'col'), may hold values from -6 to 6
- outer_product_left: bfloat16 [256, 32], replicated, may hold values from -0.375 to 0.375
- outer_product_right: bfloat16 [256, 32], replicated, may hold values from -0.375 to 0.375
- outer_proj: bfloat16 [1024, 128], replicated, may hold values from -0.1875 to 0.1875
- triangle_proj: bfloat16 [128, 512], replicated, may hold values from -0.5 to 0.5
- triangle_gate: bfloat16 [128, 128], replicated, may hold values from -0.5 to 0.5
- triangle_out: bfloat16 [128, 128], replicated, may hold values from -0.5 to 0.5
- transition_in: bfloat16 [128, 512], replicated, may hold values from -0.5 to 0.5
- transition_out: bfloat16 [512, 128], replicated, may hold values from -0.25 to 0.25
Outputs:
- pair_out: bfloat16 [192, 192, 128], P('row', 'col')
The draws below stay inside these ranges and needn't reach their ends.
Inputs may be any that keep to these rules, and one draw needn't show every extreme that they name: `residue_mask`: masked residues scattered anywhere; at least one residue is masked and at least one takes part. `alignment_mask`: 0 wherever residue_mask is 0.
All inputs are finite; a program needn't handle non-finite values.
Results may differ from the reference program's by a relative error of at most 0.014.
Values may be sent and summed in bfloat16 or wider, within the bound.
No kernel may reach another device: no remote copies, remote signals or barrier semaphores. Data moves between devices by JAX's collectives and lax.ppermute only.
A program may use at most 64 MiB of HBM per device.

```python
import jax
import jax.numpy as jnp
from jax import lax

ALIGN_CHANNELS = 256
PAIR_WIDTH = 128
OUTER_CHANNELS = 32
TRI_WIDTH = 128
TRANS_WIDTH = 512
RES_ROW = 24
SEQUENCE_COUNT = 256
RESIDUE_COUNT = 192
N_ROW = 8


def masks_together(key):
    residue_flips = jax.random.randint(jax.random.fold_in(key, 7), (RESIDUE_COUNT,), 0, 8)
    residue_part = (residue_flips < 7).astype(jnp.int32)
    zero_place = jax.random.randint(jax.random.fold_in(key, 13), (), 0, RESIDUE_COUNT)
    offset_place = jax.random.randint(jax.random.fold_in(key, 17), (), 1, RESIDUE_COUNT)
    one_place = (zero_place + offset_place) % RESIDUE_COUNT
    positions = jnp.arange(RESIDUE_COUNT, dtype=jnp.int32)
    residue_part = jnp.where(positions == one_place, jnp.int32(1), residue_part)
    residue_part = jnp.where(positions == zero_place, jnp.int32(0), residue_part).astype(jnp.int32)
    coin_flips = jax.random.randint(jax.random.fold_in(key, 11), (SEQUENCE_COUNT, RESIDUE_COUNT), 0, 20)
    present = (coin_flips < 17).astype(jnp.int32) * residue_part[None, :]
    return (residue_part, present)


def draw_residue_mask(key, part):
    return masks_together(key)[0]


def draw_alignment_mask(key, part):
    return masks_together(key)[1]


def draw_alignment(key, part):
    sequence_profile = jax.random.normal(jax.random.fold_in(key, 1), (1, RESIDUE_COUNT, ALIGN_CHANNELS), jnp.float32)
    random_jitter = jax.random.normal(jax.random.fold_in(key, 2), (SEQUENCE_COUNT, RESIDUE_COUNT, ALIGN_CHANNELS), jnp.float32)
    values = 0.8 * sequence_profile + 0.7 * random_jitter
    return jnp.clip(values, -8.0, 8.0).astype(jnp.bfloat16)


def levels(rng, shape, pieces, least, largest):
    factor_of, own = 1.0, jax.random.fold_in(rng, 6)
    for dim, blocks in pieces:
        heights = jnp.exp(jax.random.uniform(jax.random.fold_in(own, dim), (blocks,), jnp.float32, least / len(pieces), largest / len(pieces)))
        factor_of = factor_of * jnp.repeat(heights, shape[dim] // blocks).reshape([-1 if axis == dim else 1 for axis in range(len(shape))])
    return factor_of


def gaussian(own_key, shape, deviation, reach, cuts=(), held_as=jnp.bfloat16):
    array = jax.random.normal(own_key, shape, jnp.float32) * deviation
    if len(cuts) > 0:
        array = levels(own_key, shape, cuts, -0.22, 0.18) * array
    return jnp.clip(array, min=-reach, max=reach).astype(held_as)


def setup_inputs(seed: int = 0) -> dict:
    arg_keys = jax.random.split(jax.random.key(seed), 13)
    alignment = draw_alignment(jax.random.fold_in(arg_keys[12], 71), 0)
    alignment_mask = draw_alignment_mask(jax.random.fold_in(arg_keys[12], 71), 0)
    residue_mask = draw_residue_mask(jax.random.fold_in(arg_keys[12], 71), 0)
    pair_features = gaussian(arg_keys[3], (RESIDUE_COUNT, RESIDUE_COUNT, PAIR_WIDTH), 1.0, 6.0, ((0, 8), (1, 4)))
    outer_product_left = gaussian(arg_keys[4], (ALIGN_CHANNELS, OUTER_CHANNELS), ALIGN_CHANNELS ** -0.5, 0.375)
    outer_product_right = gaussian(arg_keys[5], (ALIGN_CHANNELS, OUTER_CHANNELS), ALIGN_CHANNELS ** -0.5, 0.375)
    outer_proj = gaussian(arg_keys[6], (OUTER_CHANNELS * OUTER_CHANNELS, PAIR_WIDTH), (OUTER_CHANNELS * OUTER_CHANNELS) ** -0.5, 0.1875)
    triangle_proj = gaussian(arg_keys[7], (PAIR_WIDTH, 4 * TRI_WIDTH), PAIR_WIDTH ** -0.5, 0.5)
    triangle_gate = gaussian(arg_keys[8], (PAIR_WIDTH, PAIR_WIDTH), PAIR_WIDTH ** -0.5, 0.5)
    triangle_out = gaussian(arg_keys[9], (TRI_WIDTH, PAIR_WIDTH), TRI_WIDTH ** -0.5, 0.5)
    transition_in = gaussian(arg_keys[10], (PAIR_WIDTH, TRANS_WIDTH), PAIR_WIDTH ** -0.5, 0.5)
    transition_out = gaussian(arg_keys[11], (TRANS_WIDTH, PAIR_WIDTH), TRANS_WIDTH ** -0.5, 0.25)
    return {"alignment": alignment, "alignment_mask": alignment_mask, "residue_mask": residue_mask, "pair_features": pair_features, "outer_product_left": outer_product_left, "outer_product_right": outer_product_right, "outer_proj": outer_proj, "triangle_proj": triangle_proj, "triangle_gate": triangle_gate, "triangle_out": triangle_out, "transition_in": transition_in, "transition_out": transition_out}


epsilon = 1e-05

def normalize(values):
    mean_value = lax.optimization_barrier(jnp.mean(values, axis=-1, keepdims=True))
    centered = values - mean_value
    variance = lax.optimization_barrier(jnp.mean(centered * centered, axis=-1, keepdims=True))
    return centered * lax.rsqrt(variance + epsilon)

def reference(alignment, alignment_mask, residue_mask, pair_features, outer_product_left, outer_product_right, outer_proj, triangle_proj, triangle_gate, triangle_out, transition_in, transition_out):
    mask_float = alignment_mask.astype(jnp.float32)
    normed = normalize(alignment.astype(jnp.float32)).astype(jnp.bfloat16)
    left_side = (jnp.dot(normed, outer_product_left, preferred_element_type=jnp.float32) * mask_float[..., None]).astype(jnp.bfloat16)
    right_side = (jnp.dot(normed, outer_product_right, preferred_element_type=jnp.float32) * mask_float[..., None]).astype(jnp.bfloat16)
    counts = jnp.dot(mask_float.T, mask_float, precision=lax.Precision.HIGHEST)
    right_float = right_side.astype(jnp.float32)

    def outer_rows(first_row):
        left_block = lax.dynamic_slice_in_dim(left_side, first_row, RES_ROW, 1).astype(jnp.float32)
        outer = jnp.einsum('sic,sjd->ijcd', left_block, right_float, precision=lax.Precision.HIGHEST)
        outer = outer.astype(jnp.bfloat16).reshape(RES_ROW, RESIDUE_COUNT, OUTER_CHANNELS * OUTER_CHANNELS)
        return jnp.dot(outer, outer_proj, preferred_element_type=jnp.float32)
    row_starts = jnp.arange(N_ROW, dtype=jnp.int32) * RES_ROW
    projected = lax.map(outer_rows, row_starts).reshape(RESIDUE_COUNT, RESIDUE_COUNT, PAIR_WIDTH)
    first = (pair_features.astype(jnp.float32) + projected / jnp.maximum(counts, 1.0)[..., None]).astype(jnp.bfloat16)
    normed_pair = normalize(first.astype(jnp.float32)).astype(jnp.bfloat16)
    projections = jnp.dot(normed_pair, triangle_proj, preferred_element_type=jnp.float32)
    residue_float = residue_mask.astype(jnp.float32)
    pair_mask = (residue_float[:, None] * residue_float[None, :])[..., None]
    width = TRI_WIDTH
    left_tri = (jax.nn.sigmoid(projections[..., :width]) * projections[..., width:2 * width] * pair_mask).astype(jnp.bfloat16)
    right_tri = (jax.nn.sigmoid(projections[..., 2 * width:3 * width]) * projections[..., 3 * width:] * pair_mask).astype(jnp.bfloat16)
    summed = jnp.einsum('ikc,jkc->ijc', left_tri.astype(jnp.float32), right_tri.astype(jnp.float32), precision=lax.Precision.HIGHEST)
    normed_sum = normalize(summed).astype(jnp.bfloat16)
    update = jax.nn.sigmoid(jnp.dot(normed_pair, triangle_gate, preferred_element_type=jnp.float32)) * jnp.dot(normed_sum, triangle_out, preferred_element_type=jnp.float32)
    second = (first.astype(jnp.float32) + update).astype(jnp.bfloat16)
    normed_second = normalize(second.astype(jnp.float32)).astype(jnp.bfloat16)
    hidden_units = jnp.maximum(jnp.dot(normed_second, transition_in, preferred_element_type=jnp.float32), 0.0).astype(jnp.bfloat16)
    return (second.astype(jnp.float32) + jnp.dot(hidden_units, transition_out, preferred_element_type=jnp.float32)).astype(jnp.bfloat16)
```

```python
import functools

import jax
import jax.numpy as jnp
from jax import lax
from jax.experimental import pallas as pl
from jax.experimental.pallas import tpu as pltpu
from jax.sharding import PartitionSpec as P

epsilon = 1e-05
LANES = 128
BF16 = jnp.bfloat16
F32 = jnp.float32
NT = (((1,), (1,)), ((), ()))
TN = (((0,), (0,)), ((), ()))


def matmul(a, b, dims=(((1,), (0,)), ((), ()))):
    return lax.dot_general(a, b, dims, preferred_element_type=F32)


def iota(shape, axis):
    return lax.broadcasted_iota(jnp.int32, shape, axis)


def normalize(values, axis=-1):
    mean_value = jnp.mean(values, axis=axis, keepdims=True)
    centered = values - mean_value
    variance = jnp.mean(centered * centered, axis=axis, keepdims=True)
    return centered * lax.rsqrt(variance + epsilon)


def params(cost=None):
    return dict(
        compiler_params=pltpu.CompilerParams(vmem_limit_bytes=56 * 1024 * 1024),
        cost_estimate=cost,
    )


VMEM = pl.BlockSpec(memory_space=pltpu.VMEM)
SMEM = pl.BlockSpec(memory_space=pltpu.SMEM)


def side_kernel(
    sequences, cols, half, copies, narrow,
    index_ref, align_ref, mask_ref, left_w_ref, right_w_ref,
    right_ref, left_ref, left_projected, right_projected,
):
    members = LANES // narrow
    rows = sequences * cols
    chunk = rows // 12 if rows % (12 * 16) == 0 else rows
    left_w = jnp.concatenate([left_w_ref[...]] * members, axis=1)
    right_w = jnp.concatenate([right_w_ref[...]] * members, axis=1)

    def project(step, carry):
        start = pl.multiple_of(step * chunk, chunk)
        normed = normalize(align_ref[pl.ds(start, chunk), :].astype(F32)).astype(BF16)
        left_projected[pl.ds(start, chunk), :] = matmul(normed, left_w)
        right_projected[pl.ds(start, chunk), :] = matmul(normed, right_w)
        return carry

    lax.fori_loop(0, rows // chunk, project, 0)
    mask = mask_ref[...].astype(BF16)
    lane = iota((sequences, LANES), 1)

    def group_of(projected, first, groups, group):
        value = None
        for member in range(members):
            j = first + member * groups + group
            part = projected[pl.ds(j, sequences, stride=cols), :]
            value = part if value is None else jnp.where(lane >= member * narrow, part, value)
        return value

    def spread(first, groups):
        width = groups * LANES
        at = iota((cols, width), 1)
        residue = first + (at % LANES) // narrow * groups + at // LANES
        return matmul(mask, (iota((cols, width), 0) == residue).astype(BF16))

    def mask_lanes(first, count):
        pick = iota((cols, LANES), 0) - first == iota((cols, LANES), 1)
        pick = pick & (iota((cols, LANES), 1) < count)
        return matmul(mask, pick.astype(BF16)).astype(BF16)

    groups = cols // members
    masks = spread(0, groups)
    for group in range(groups):
        at = slice(group * LANES, (group + 1) * LANES)
        value = (group_of(right_projected, 0, groups, group) * masks[:, at]).astype(BF16)
        for copy in range(copies):
            right_ref[copy, :, at] = value
    tail = mask_lanes(0, cols)
    for copy in range(copies):
        right_ref[copy, :, groups * LANES :] = tail
    halves = cols // half
    groups = half // members
    turn = index_ref[0]
    for h in range(halves):
        place = lax.rem(h - turn + halves, halves)
        masks = spread(h * half, groups)
        for group in range(groups):
            at = slice(group * LANES, (group + 1) * LANES)
            value = group_of(left_projected, h * half, groups, group) * masks[:, at]
            left_ref[place, :, at] = value.astype(BF16)
        left_ref[place, :, groups * LANES :] = mask_lanes(h * half, half)


def outer_kernel(
    rows, cols, narrow, width, turns,
    index_ref, left_ref, right_ref, pair_ref, proj_ref, tri_ref, pair_mask_ref,
    first_ref, normed_ref, tri_out_ref, left_t, stacked, spread_w, moved,
):
    members = LANES // narrow
    left_groups, groups = rows // members, cols // members
    left_width, right_width = rows * narrow, cols * narrow
    sources = left_ref.shape[0]
    h = index_ref[0]
    left = jnp.concatenate(
        [left_ref[c, lax.rem(h - t + turns, turns)] for c in range(sources) for t in range(turns)], axis=0
    )
    right_mask = right_ref[:, right_width:]
    left_mask = left[:, left_width:]
    left = left[:, :left_width]
    at = iota((left_width, left_width), 0)
    channel, residue = at // rows, at % rows
    column = residue % left_groups * LANES + residue // left_groups * narrow + channel
    pick = (iota((left_width, left_width), 1) == column).astype(BF16)
    left_t[...] = matmul(pick, left, NT).astype(BF16)
    spread_w[...] = jnp.zeros_like(spread_w)
    for c in range(narrow):
        part = proj_ref[c * narrow : (c + 1) * narrow, :]
        for m in range(members):
            start = c * LANES + m * narrow
            spread_w[start : start + narrow, m * width : (m + 1) * width] = part
    step = 8
    for first in range(0, narrow, step):
        block = matmul(left_t[first * rows : (first + step) * rows, :], right_ref[:, :right_width])
        for c in range(step):
            lanes = slice((first + c) * LANES, (first + c + 1) * LANES)
            for g in range(0, groups, 2):
                two = [
                    block[c * rows : (c + 1) * rows, (g + n) * LANES : (g + n + 1) * LANES] for n in range(2)
                ]
                stacked[g * rows : (g + 2) * rows, lanes] = jnp.concatenate(two, axis=0).astype(BF16)
    total = matmul(stacked[...], spread_w[...])
    counts = matmul(left_mask, right_mask, TN)[:rows, :]
    scale = 1.0 / jnp.maximum(counts, 1.0)
    for m in range(members):
        for g in range(groups):
            j = m * groups + g
            part = total[g * rows : (g + 1) * rows, m * width : (m + 1) * width]
            moved[j * rows : (j + 1) * rows, :] = part * scale[:, j : j + 1]
    for i in range(rows):
        at = slice(i * cols, (i + 1) * cols)
        first = pair_ref[at, :].astype(F32) + moved[pl.ds(i, cols, stride=rows), :]
        first = first.astype(BF16)
        first_ref[at, :] = first
        normed_ref[at, :] = normalize(first.astype(F32)).astype(BF16)
    devices = tri_out_ref.shape[0]
    own = width // devices
    at = iota((4 * width, 4 * width), 0)
    kind, rest = at // (2 * width), at % (2 * width)
    owner, side, channel = rest // (2 * own), rest // own % 2, rest % own
    column = side * 2 * width + kind * width + owner * own + channel
    pick = (iota((4 * width, 4 * width), 1) == column).astype(BF16)
    weights = matmul(pick, tri_ref[...], NT).astype(BF16)
    projections = matmul(weights, normed_ref[...], NT)
    gated = jax.nn.sigmoid(projections[: 2 * width]) * projections[2 * width :] * pair_mask_ref[...]
    gated = gated.astype(BF16)
    for d in range(devices):
        tri_out_ref[d] = gated[d * 2 * own : (d + 1) * 2 * own, :]


def triangle_kernel(row_count, col_count, rows, cols, own, given_ref, out_ref, opened, summed):
    residues = row_count * rows
    pair = 2 * own
    planes = opened.shape[0]
    each = -(-col_count // planes)

    def open_row(r, carry):
        for c in range(col_count):
            value = given_ref[r * col_count + c].astype(F32)
            lanes = slice(c % each * cols, (c % each + 1) * cols)
            for i in range(rows):
                start = pl.multiple_of((r * rows + i) * pair, pair)
                opened[c // each, pl.ds(start, pair), lanes] = value[:, i * cols : (i + 1) * cols]
        return carry

    lax.fori_loop(0, row_count, open_row, 0)
    used = each * cols
    for t in range(own):
        left = [opened.at[p][pl.ds(t, residues, stride=pair), :].astype(BF16) for p in range(planes)]
        right = [opened.at[p][pl.ds(own + t, residues, stride=pair), :].astype(BF16) for p in range(planes)]
        for q in range(planes):
            total = None
            for p in range(planes):
                width = min(each, col_count - p * each) * cols
                some = right[p][q * used : min((q + 1) * used, residues), :width]
                if some.shape[0] < LANES:
                    some = jnp.concatenate([some, jnp.zeros((LANES - some.shape[0], width), BF16)], axis=0)
                term = matmul(left[p][:, :width], some, NT)
                total = term if total is None else total + term
            summed.at[q][pl.ds(t, residues, stride=pair), :] = total

    def close_row(r, carry):
        for c in range(col_count):
            lanes = slice(c % each * cols, (c % each + 1) * cols)
            parts = []
            for i in range(rows):
                start = pl.multiple_of((r * rows + i) * pair, pair)
                parts.append(summed[c // each, pl.ds(start, pair), lanes])
            out_ref[r * col_count + c] = jnp.concatenate(parts, axis=1)[:own].astype(BF16)
        return carry

    lax.fori_loop(0, row_count, close_row, 0)


def triangle_by_channel(row_count, col_count, rows, cols, gated):
    devices, pair, places = gated.shape
    own = pair // 2
    gated = lax.all_to_all(gated, ("row", "col"), split_axis=0, concat_axis=0, tiled=True)
    residues = row_count * rows
    planes = -(-col_count // (LANES // cols))
    summed = pl.pallas_call(
        functools.partial(triangle_kernel, row_count, col_count, rows, cols, own),
        out_shape=jax.ShapeDtypeStruct((devices, own, places), BF16),
        in_specs=[VMEM],
        out_specs=VMEM,
        scratch_shapes=[pltpu.VMEM((planes, residues * 2 * own, LANES), F32)] * 2,
        **params(),
    )(gated)
    summed = lax.all_to_all(summed, ("row", "col"), split_axis=0, concat_axis=0, tiled=True)
    return summed.reshape(devices * own, places)


def triangle_by_residue(row_count, col_count, rows, cols, gated):
    _, pair, places = gated.shape
    both = gated.reshape(2, pair // 2, rows, cols).transpose(0, 2, 3, 1)
    right = lax.all_gather(both[1], "row", axis=0, tiled=True)
    right = lax.all_to_all(right, "col", split_axis=0, concat_axis=1, tiled=True)
    left = lax.all_gather(both[0], "col", axis=1, tiled=True)
    summed = jnp.einsum("ikc,jkc->cij", left, right, preferred_element_type=F32)
    return summed.reshape(pair // 2, places).astype(BF16)


def tail_kernel(first_ref, normed_ref, summed_ref, gate_ref, out_w_ref, in_ref, back_ref, out_ref):
    normed_sum = normalize(summed_ref[...].astype(F32), 0).astype(BF16)
    gate = jax.nn.sigmoid(matmul(gate_ref[...].T, normed_ref[...], NT))
    update = gate * matmul(out_w_ref[...].T, normed_sum)
    second = (first_ref[...].astype(F32).T + update).astype(BF16).astype(F32)
    normed_second = normalize(second, 0).astype(BF16)
    hidden = jnp.maximum(matmul(in_ref[...].T, normed_second), 0.0).astype(BF16)
    result = second + matmul(back_ref[...].T, hidden)
    out_ref[...] = result.T.astype(BF16)


def shards(
    row_count, col_count, alignment, alignment_mask, residue_mask, pair_features, outer_product_left, outer_product_right,
    outer_proj, triangle_proj, triangle_gate, triangle_out, transition_in, transition_out,
):
    rows, cols, width = pair_features.shape
    sequences, _, channels = alignment.shape
    narrow = outer_product_left.shape[1]
    inner = triangle_out.shape[0]
    devices = row_count * col_count
    turns = cols // rows
    places = rows * cols
    r, c = lax.axis_index("row"), lax.axis_index("col")
    turn = (r % turns).astype(jnp.int32).reshape(1)

    members = LANES // narrow
    right_lanes = cols * narrow + LANES
    left_lanes = rows * narrow + LANES
    right, left = pl.pallas_call(
        functools.partial(side_kernel, sequences, cols, rows, row_count, narrow),
        out_shape=(
            jax.ShapeDtypeStruct((row_count, sequences, right_lanes), BF16),
            jax.ShapeDtypeStruct((turns, sequences, left_lanes), BF16),
        ),
        in_specs=[SMEM] + [VMEM] * 4,
        out_specs=(VMEM, VMEM),
        scratch_shapes=[pltpu.VMEM((sequences * cols, LANES), F32)] * 2,
        **params(),
    )(turn, alignment.reshape(sequences * cols, channels), alignment_mask, outer_product_left, outer_product_right)

    sent = []
    for p in range(turns):
        route = []
        for source_row in range(row_count):
            for source_col in range(col_count):
                to_row = turns * source_col + (source_row + p) % turns
                route.append((source_row * col_count + source_col, to_row * col_count + source_row // turns))
        sent.append(lax.ppermute(left[p], ("row", "col"), route))
    left = jnp.stack(sent)
    left = lax.all_to_all(
        jnp.broadcast_to(left[None], (col_count,) + left.shape), "col", split_axis=0, concat_axis=0, tiled=True
    )
    right = lax.all_to_all(right, "row", split_axis=0, concat_axis=0, tiled=True)
    right = right.reshape(row_count * sequences, right_lanes)

    residue_float = residue_mask.astype(F32)
    row_mask = lax.dynamic_slice_in_dim(residue_float, r * rows, rows)
    col_mask = lax.dynamic_slice_in_dim(residue_float, c * cols, cols)
    pair_mask = (row_mask[:, None] * col_mask[None, :]).reshape(1, places)

    by_channel = inner % devices == 0
    owners = devices if by_channel else 1
    own = inner // owners
    first, normed_pair, gated = pl.pallas_call(
        functools.partial(outer_kernel, rows, cols, narrow, width, turns),
        out_shape=(
            jax.ShapeDtypeStruct((places, width), BF16),
            jax.ShapeDtypeStruct((places, width), BF16),
            jax.ShapeDtypeStruct((owners, 2 * own, places), BF16),
        ),
        in_specs=[SMEM] + [VMEM] * 6,
        out_specs=(VMEM,) * 3,
        scratch_shapes=[
            pltpu.VMEM((rows * narrow, row_count * sequences), BF16),
            pltpu.VMEM((cols // members * rows, narrow * LANES), BF16),
            pltpu.VMEM((narrow * LANES, members * width), BF16),
            pltpu.VMEM((places, width), F32),
        ],
        **params(),
    )(turn, left, right, pair_features.reshape(places, width), outer_proj, triangle_proj, pair_mask)

    triangle = triangle_by_channel if by_channel else triangle_by_residue
    summed = triangle(row_count, col_count, rows, cols, gated)
    out = pl.pallas_call(
        tail_kernel,
        out_shape=jax.ShapeDtypeStruct((places, width), BF16),
        in_specs=[VMEM] * 7,
        out_specs=VMEM,
        **params(),
    )(first, normed_pair, summed, triangle_gate, triangle_out, transition_in, transition_out)
    return out.reshape(rows, cols, width)


def solution(mesh):
    placed = (
        P("row", "col", None),
        P("row", "col"),
        P(),
        P("row", "col", None),
    ) + (P(),) * 8
    body = functools.partial(shards, mesh.shape["row"], mesh.shape["col"])
    return jax.shard_map(body, mesh=mesh, in_specs=placed, out_specs=P("row", "col", None), check_vma=False)
```

```python
import functools

import jax
import jax.numpy as jnp
from jax import lax
from jax.experimental import pallas as pl
from jax.experimental.pallas import tpu as pltpu
from jax.sharding import PartitionSpec as P


epsilon = 1e-05
LANES = 128
BF16 = jnp.bfloat16
F32 = jnp.float32
NT = (((1,), (1,)), ((), ()))
TN = (((0,), (0,)), ((), ()))


def matmul(a, b, dims=(((1,), (0,)), ((), ()))):
    return lax.dot_general(a, b, dims, preferred_element_type=F32)


def iota(shape, axis):
    return lax.broadcasted_iota(jnp.int32, shape, axis)


def normalize(values, axis=-1):
    mean_value = jnp.mean(values, axis=axis, keepdims=True)
    centered = values - mean_value
    variance = jnp.mean(centered * centered, axis=axis, keepdims=True)
    return centered * lax.rsqrt(variance + epsilon)


def params(mebibytes):
    return dict(compiler_params=pltpu.CompilerParams(vmem_limit_bytes=mebibytes * 1024 * 1024))


VMEM = pl.BlockSpec(memory_space=pltpu.VMEM)
SMEM = pl.BlockSpec(memory_space=pltpu.SMEM)


def side_kernel(sequences, cols, parts, copies, narrow, index_ref, align_ref, mask_ref, weights_ref, *refs):
    *out_refs, projected = refs
    members = LANES // narrow
    rows = sequences * cols
    chunk = rows // 12 if rows % (12 * 16) == 0 else rows
    weights = jnp.concatenate([weights_ref[...]] * members, axis=0)

    def project(step, carry):
        start = pl.multiple_of(step * chunk, chunk)
        normed = normalize(align_ref[pl.ds(start, chunk), :].astype(F32)).astype(BF16)
        projected[pl.ds(start, chunk), :] = matmul(normed, weights, NT)
        return carry

    lax.fori_loop(0, rows // chunk, project, 0)
    mask = mask_ref[...].astype(BF16)
    lane = iota((sequences, LANES), 1)
    count = cols // parts
    groups = count // members
    width = groups * LANES
    for h in range(parts):
        first = h * count
        at = iota((cols, width), 1)
        residue = first + (at % LANES) // narrow * groups + at // LANES
        masks = matmul(mask, (iota((cols, width), 0) == residue).astype(BF16))
        values = []
        for group in range(groups):
            value = None
            for member in range(members):
                part = projected[pl.ds(first + member * groups + group, sequences, stride=cols), :]
                value = part if value is None else jnp.where(lane >= member * narrow, part, value)
            values.append((value * masks[:, group * LANES : (group + 1) * LANES]).astype(BF16))
        at = iota((cols, LANES), 1)
        pick = (iota((cols, LANES), 0) - first == at) & (at < count)
        values.append(matmul(mask, pick.astype(BF16)).astype(BF16))
        for p in range(parts):

            @pl.when(lax.rem(index_ref[0] + p, parts) == h)
            def _():
                for group, value in enumerate(values):
                    lanes = slice(group * LANES, (group + 1) * LANES)
                    for copy in range(copies):
                        out_refs[p][copy, :, lanes] = value


def outer_kernel(
    rows, cols, narrow, width, turns, sources,
    index_ref, *refs,
):
    left_refs, refs = refs[:sources], refs[sources:]
    right_ref, pair_ref, proj_ref, tri_ref, pair_mask_ref, first_ref, normed_ref, tri_out_ref = refs[:8]
    gathered, left_t, stacked, spread_w, moved = refs[8:]
    members = LANES // narrow
    left_groups, groups = rows // members, cols // members
    left_width, right_width = rows * narrow, cols * narrow
    h, column = index_ref[0], index_ref[1]
    block = left_refs[0].shape[1]
    for k, left_ref in enumerate(left_refs):
        for t in range(turns):
            start = (source(column, k, sources) * turns + t) * block
            gathered[pl.ds(pl.multiple_of(start, block), block), :] = left_ref[lax.rem(h - t + turns, turns)]
    left = gathered[...]
    right_mask = right_ref[:, right_width:]
    left_mask = left[:, left_width:]
    left = left[:, :left_width]
    at = iota((left_width, left_width), 0)
    channel, residue = at // rows, at % rows
    column = residue % left_groups * LANES + residue // left_groups * narrow + channel
    pick = (iota((left_width, left_width), 1) == column).astype(BF16)
    left_t[...] = matmul(pick, left, NT).astype(BF16)
    spread_w[...] = jnp.zeros_like(spread_w)
    for c in range(narrow):
        part = proj_ref[c * narrow : (c + 1) * narrow, :]
        for m in range(members):
            start = c * LANES + m * narrow
            spread_w[start : start + narrow, m * width : (m + 1) * width] = part
    step = 8
    for first in range(0, narrow, step):
        block = matmul(left_t[first * rows : (first + step) * rows, :], right_ref[:, :right_width])
        for c in range(step):
            lanes = slice((first + c) * LANES, (first + c + 1) * LANES)
            for g in range(0, groups, 2):
                two = [
                    block[c * rows : (c + 1) * rows, (g + n) * LANES : (g + n + 1) * LANES] for n in range(2)
                ]
                stacked[g * rows : (g + 2) * rows, lanes] = jnp.concatenate(two, axis=0).astype(BF16)
    total = matmul(stacked[...], spread_w[...])
    counts = matmul(left_mask, right_mask, TN)[:rows, :]
    scale = 1.0 / jnp.maximum(counts, 1.0)
    for m in range(members):
        for g in range(groups):
            j = m * groups + g
            part = total[g * rows : (g + 1) * rows, m * width : (m + 1) * width]
            moved[j * rows : (j + 1) * rows, :] = part * scale[:, j : j + 1]
    for i in range(rows):
        at = slice(i * cols, (i + 1) * cols)
        first = pair_ref[at, :].astype(F32) + moved[pl.ds(i, cols, stride=rows), :]
        first = first.astype(BF16)
        first_ref[at, :] = first
        normed_ref[at, :] = normalize(first.astype(F32)).astype(BF16)
    devices = tri_out_ref.shape[0]
    own = width // devices
    at = iota((4 * width, 4 * width), 0)
    kind, rest = at // (2 * width), at % (2 * width)
    owner, side, channel = rest // (2 * own), rest // own % 2, rest % own
    column = side * 2 * width + kind * width + owner * own + channel
    pick = (iota((4 * width, 4 * width), 1) == column).astype(BF16)
    weights = matmul(pick, tri_ref[...], NT).astype(BF16)
    projections = matmul(weights, normed_ref[...], NT)
    gated = jax.nn.sigmoid(projections[: 2 * width]) * projections[2 * width :] * pair_mask_ref[...]
    gated = gated.astype(BF16)
    for d in range(devices):
        tri_out_ref[d] = gated[d * 2 * own : (d + 1) * 2 * own, :]


def triangle_kernel(row_count, col_count, rows, cols, own, given_ref, out_ref, opened, summed):
    residues = row_count * rows
    pair = 2 * own
    planes = opened.shape[0]
    each = -(-col_count // planes)

    def open_row(r, carry):
        for c in range(col_count):
            value = given_ref[r * col_count + c].astype(F32)
            lanes = slice(c % each * cols, (c % each + 1) * cols)
            for i in range(rows):
                start = pl.multiple_of((r * rows + i) * pair, pair)
                opened[c // each, pl.ds(start, pair), lanes] = value[:, i * cols : (i + 1) * cols]
        return carry

    lax.fori_loop(0, row_count, open_row, 0)
    used = each * cols
    for t in range(own):
        left = [opened.at[p][pl.ds(t, residues, stride=pair), :].astype(BF16) for p in range(planes)]
        right = [opened.at[p][pl.ds(own + t, residues, stride=pair), :].astype(BF16) for p in range(planes)]
        for q in range(planes):
            total = None
            for p in range(planes):
                width = min(each, col_count - p * each) * cols
                some = right[p][q * used : min((q + 1) * used, residues), :width]
                if some.shape[0] < LANES:
                    some = jnp.concatenate([some, jnp.zeros((LANES - some.shape[0], width), BF16)], axis=0)
                term = matmul(left[p][:, :width], some, NT)
                total = term if total is None else total + term
            summed.at[q][pl.ds(t, residues, stride=pair), :] = total

    def close_row(r, carry):
        for c in range(col_count):
            lanes = slice(c % each * cols, (c % each + 1) * cols)
            parts = []
            for i in range(rows):
                start = pl.multiple_of((r * rows + i) * pair, pair)
                parts.append(summed[c // each, pl.ds(start, pair), lanes])
            out_ref[r * col_count + c] = jnp.concatenate(parts, axis=1)[:own].astype(BF16)
        return carry

    lax.fori_loop(0, row_count, close_row, 0)


def partner(index, k, count):
    return index ^ k if count & (count - 1) == 0 else (index + k) % count


def source(index, k, count):
    return index ^ k if count & (count - 1) == 0 else lax.rem(index - k + count, count)


def triangle_by_channel(row_count, col_count, rows, cols, gated):
    devices, pair, places = gated.shape
    own = pair // 2
    gated = lax.all_to_all(gated, ("row", "col"), split_axis=0, concat_axis=0, tiled=True)
    residues = row_count * rows
    planes = -(-col_count // (LANES // cols))
    summed = pl.pallas_call(
        functools.partial(triangle_kernel, row_count, col_count, rows, cols, own),
        out_shape=jax.ShapeDtypeStruct((devices, own, places), BF16),
        in_specs=[VMEM],
        out_specs=VMEM,
        scratch_shapes=[pltpu.VMEM((planes, residues * 2 * own, LANES), F32)] * 2,
        **params(24),
    )(gated)
    summed = lax.all_to_all(summed, ("row", "col"), split_axis=0, concat_axis=0, tiled=True)
    return summed


def triangle_by_residue(row_count, col_count, rows, cols, gated):
    _, pair, places = gated.shape
    both = gated.reshape(2, pair // 2, rows, cols).transpose(0, 2, 3, 1)
    right = lax.all_gather(both[1], "row", axis=0, tiled=True)
    right = lax.all_to_all(right, "col", split_axis=0, concat_axis=1, tiled=True)
    left = lax.all_gather(both[0], "col", axis=1, tiled=True)
    summed = jnp.einsum("ikc,jkc->cij", left, right, preferred_element_type=F32)
    return summed.reshape(1, pair // 2, places).astype(BF16)


def tail_kernel(first_ref, normed_ref, summed_ref, gate_ref, out_w_ref, in_ref, back_ref, out_ref, summed):
    own = summed_ref.shape[1]
    for d in range(summed_ref.shape[0]):
        summed[d * own : (d + 1) * own, :] = summed_ref[d].astype(F32)
    normed_sum = normalize(summed[...], 0).astype(BF16)
    gate = jax.nn.sigmoid(matmul(gate_ref[...].T, normed_ref[...], NT))
    update = gate * matmul(out_w_ref[...].T, normed_sum)
    second = (first_ref[...].astype(F32).T + update).astype(BF16).astype(F32)
    normed_second = normalize(second, 0).astype(BF16)
    hidden = jnp.maximum(matmul(in_ref[...].T, normed_second), 0.0).astype(BF16)
    result = second + matmul(back_ref[...].T, hidden)
    out_ref[...] = result.T.astype(BF16)


def shards(
    row_count, col_count, alignment, alignment_mask, residue_mask, pair_features, outer_product_left, outer_product_right,
    outer_proj, triangle_proj, triangle_gate, triangle_out, transition_in, transition_out,
):
    rows, cols, width = pair_features.shape
    sequences, _, channels = alignment.shape
    narrow = outer_product_left.shape[1]
    inner = triangle_out.shape[0]
    devices = row_count * col_count
    turns = cols // rows
    places = rows * cols
    r, c = lax.axis_index("row"), lax.axis_index("col")
    place = jnp.stack([r % turns, c]).astype(jnp.int32)

    members = LANES // narrow
    right_lanes = cols * narrow + LANES
    left_lanes = rows * narrow + LANES

    def side(weights, parts, copies):
        shape = (copies, sequences, cols // parts * narrow + LANES)
        return pl.pallas_call(
            functools.partial(side_kernel, sequences, cols, parts, copies, narrow),
            out_shape=(jax.ShapeDtypeStruct(shape, BF16),) * parts,
            in_specs=[SMEM] + [VMEM] * 3,
            out_specs=(VMEM,) * parts,
            scratch_shapes=[pltpu.VMEM((sequences * cols, LANES), F32)],
            **params(12),
        )(place, alignment.reshape(sequences * cols, channels), alignment_mask, weights.T)

    left = side(outer_product_left, turns, 1)
    (right,) = side(outer_product_right, 1, row_count)

    right = lax.all_to_all(right, "row", split_axis=0, concat_axis=0, tiled=True)
    right = right.reshape(row_count * sequences, right_lanes)
    sent = []
    for p in range(turns):
        route = []
        for source_row in range(row_count):
            for source_col in range(col_count):
                to_row = turns * source_col + (source_row + p) % turns
                route.append((source_row * col_count + source_col, to_row * col_count + source_row // turns))
        sent.append(lax.ppermute(left[p][0], ("row", "col"), route))
    left = jnp.stack(sent)
    lefts = [left]
    for k in range(1, col_count):
        lefts.append(lax.ppermute(left, "col", [(col, partner(col, k, col_count)) for col in range(col_count)]))

    residue_float = residue_mask.astype(F32)
    row_mask = lax.dynamic_slice_in_dim(residue_float, r * rows, rows)
    col_mask = lax.dynamic_slice_in_dim(residue_float, c * cols, cols)
    pair_mask = (row_mask[:, None] * col_mask[None, :]).reshape(1, places)

    by_channel = inner % devices == 0
    owners = devices if by_channel else 1
    own = inner // owners
    first, normed_pair, gated = pl.pallas_call(
        functools.partial(outer_kernel, rows, cols, narrow, width, turns, col_count),
        out_shape=(
            jax.ShapeDtypeStruct((places, width), BF16),
            jax.ShapeDtypeStruct((places, width), BF16),
            jax.ShapeDtypeStruct((owners, 2 * own, places), BF16),
        ),
        in_specs=[SMEM] + [VMEM] * (5 + col_count),
        out_specs=(VMEM,) * 3,
        scratch_shapes=[
            pltpu.VMEM((row_count * sequences, left_lanes), BF16),
            pltpu.VMEM((rows * narrow, row_count * sequences), BF16),
            pltpu.VMEM((cols // members * rows, narrow * LANES), BF16),
            pltpu.VMEM((narrow * LANES, members * width), BF16),
            pltpu.VMEM((places, width), F32),
        ],
        **params(16),
    )(place, *lefts, right, pair_features.reshape(places, width), outer_proj, triangle_proj, pair_mask)

    triangle = triangle_by_channel if by_channel else triangle_by_residue
    summed = triangle(row_count, col_count, rows, cols, gated)
    out = pl.pallas_call(
        tail_kernel,
        out_shape=jax.ShapeDtypeStruct((places, width), BF16),
        in_specs=[VMEM] * 7,
        out_specs=VMEM,
        scratch_shapes=[pltpu.VMEM((inner, places), F32)],
        **params(16),
    )(first, normed_pair, summed, triangle_gate, triangle_out, transition_in, transition_out)
    return out.reshape(rows, cols, width)


def solution(mesh):
    placed = (
        P("row", "col", None),
        P("row", "col"),
        P(),
        P("row", "col", None),
    ) + (P(),) * 8

    def body(*args):
        return shards(mesh.shape["row"], mesh.shape["col"], *args)

    return jax.shard_map(body, mesh=mesh, in_specs=placed, out_specs=P("row", "col", None), check_vma=False)
```

```python
import functools

import jax
import jax.numpy as jnp
from jax import lax
from jax.experimental import pallas as pl
from jax.experimental.pallas import tpu as pltpu
from jax.sharding import PartitionSpec as P


epsilon = 1e-05
LANES = 128
BF16 = jnp.bfloat16
F32 = jnp.float32
NT = (((1,), (1,)), ((), ()))
TN = (((0,), (0,)), ((), ()))


def matmul(a, b, dims=(((1,), (0,)), ((), ()))):
    return lax.dot_general(a, b, dims, preferred_element_type=F32)


def iota(shape, axis):
    return lax.broadcasted_iota(jnp.int32, shape, axis)


def normalize(values, axis=-1):
    mean_value = jnp.mean(values, axis=axis, keepdims=True)
    centered = values - mean_value
    variance = jnp.mean(centered * centered, axis=axis, keepdims=True)
    return centered * lax.rsqrt(variance + epsilon)


def in_hbm(values):
    return [pltpu.with_memory_space_constraint(value, pltpu.HBM) for value in values]


def call(kernel, mebibytes, outs, scratch, in_specs=None, out_specs=None):
    return pl.pallas_call(
        kernel,
        out_shape=tuple(jax.ShapeDtypeStruct(*out) for out in outs),
        out_specs=out_specs or (VMEM,) * len(outs),
        scratch_shapes=scratch,
        compiler_params=pltpu.CompilerParams(vmem_limit_bytes=mebibytes * 1024 * 1024),
        **({} if in_specs is None else {"in_specs": in_specs}),
    )


VMEM = pl.BlockSpec(memory_space=pltpu.VMEM)


def pack_side(projected, mask, narrow, first, count, put):
    sequences, cols = mask.shape
    members = LANES // narrow
    lane = iota((sequences, LANES), 1)
    groups = count // members
    width = groups * LANES
    at = iota((cols, width), 1)
    residue = first + (at % LANES) // narrow * groups + at // LANES
    masks = matmul(mask, (iota((cols, width), 0) == residue).astype(BF16))
    for group in range(groups):
        value = None
        for member in range(members):
            part = projected[pl.ds(first + member * groups + group, sequences, stride=cols), :]
            value = part if value is None else jnp.where(lane >= member * narrow, part, value)
        put(group, (value * masks[:, group * LANES : (group + 1) * LANES]).astype(BF16))
    at = iota((cols, LANES), 1)
    pick = (iota((cols, LANES), 0) - first == at) & (at < count)
    put(groups, matmul(mask, pick.astype(BF16)).astype(BF16))


def side_kernel(
    chunks, narrow, align_hbm, mask_hbm, left_w_hbm, right_w_hbm, right_hbm, left_ref,
    left_rows, right_rows, align, mask_int, left_w, right_w, packed, align_sem, mask_sem, left_sem, right_sem, out_sem,
):
    chunk = align.shape[0] // chunks
    small = [
        pltpu.make_async_copy(left_w_hbm, left_w, left_sem),
        pltpu.make_async_copy(right_w_hbm, right_w, right_sem),
        pltpu.make_async_copy(mask_hbm, mask_int, mask_sem),
    ]
    parts = []
    for n in range(chunks):
        at = pl.ds(n * chunk, chunk)
        parts.append(pltpu.make_async_copy(align_hbm.at[at, :], align.at[at, :], align_sem.at[n]))
    for copy in small[:2] + parts + small[2:]:
        copy.start()
    small[0].wait()
    small[1].wait()
    members = LANES // narrow
    both = jnp.concatenate([left_w[...]] * members + [right_w[...]] * members, axis=0)
    for n in range(chunks):
        parts[n].wait()
        at = slice(n * chunk, (n + 1) * chunk)
        normed = normalize(align[at, :].astype(F32)).astype(BF16)
        value = matmul(normed, both, NT)
        left_rows[at, :] = value[:, :LANES]
        right_rows[at, :] = value[:, LANES:]
    small[2].wait()
    mask = mask_int[...].astype(BF16)
    cols = mask.shape[1]

    def put_right(group, value):
        packed[:, group * LANES : (group + 1) * LANES] = value

    pack_side(right_rows, mask, narrow, 0, cols, put_right)
    copies = [pltpu.make_async_copy(packed, right_hbm.at[n], out_sem.at[n]) for n in range(right_hbm.shape[0])]
    for copy in copies:
        copy.start()
    turns = left_ref.shape[0]
    turn = lax.rem(lax.axis_index("row"), turns)
    for h in range(turns):
        place = lax.rem(h - turn + turns, turns)

        def put_left(group, value):
            left_ref[place, :, group * LANES : (group + 1) * LANES] = value

        pack_side(left_rows, mask, narrow, h * (cols // turns), cols // turns, put_left)
    for copy in copies:
        copy.wait()


def prepare_kernel(rows, narrow, turns, sources, own, tri_ref, *refs):
    left_refs, refs = refs[: turns * sources], refs[turns * sources :]
    tri_rows_ref, left_t_ref, mask_ref, gathered = refs
    block = left_refs[0].shape[0]
    h, column = lax.rem(lax.axis_index("row"), turns), lax.axis_index("col")
    for n, left_ref in enumerate(left_refs):
        d, k = n // sources, n % sources
        start = (source(column, k, sources) * turns + lax.rem(h - d + turns, turns)) * block
        gathered[pl.ds(pl.multiple_of(start, block), block), :] = left_ref[...]
    out = tri_ref.shape[0]
    members = LANES // narrow
    width = rows * narrow
    groups = rows // members
    at = iota((width, width), 0)
    channel, residue = at // rows, at % rows
    place = residue % groups * LANES + residue // groups * narrow + channel
    pick = (iota((width, width), 1) == place).astype(BF16)
    left_t_ref[...] = matmul(pick, gathered[:, :width], NT).astype(BF16)
    mask_ref[...] = gathered[:, width:]
    at = iota((4 * out, 4 * out), 0)
    kind, rest = at // (2 * out), at % (2 * out)
    owner, side, channel = rest // (2 * own), rest // own % 2, rest % own
    column = side * 2 * out + kind * out + owner * own + channel
    pick = (iota((4 * out, 4 * out), 1) == column).astype(BF16)
    tri_rows_ref[...] = matmul(pick, tri_ref[...], NT).astype(BF16)


def outer_kernel(
    rows, cols, narrow, left_t, left_mask_ref, right_ref, tri_ref, pair_mask_ref, pair_ref, proj_ref,
    first_ref, normed_ref, tri_out_ref, stacked, spread, moved,
):
    members = LANES // narrow
    groups = cols // members
    right_width = cols * narrow
    width = pair_ref.shape[1]
    steps = stacked.shape[0]
    step = narrow // steps
    spread[...] = jnp.zeros_like(spread)
    total = None
    for first in range(0, narrow, step):
        block = matmul(left_t[first * rows : (first + step) * rows, :], right_ref[:, :right_width])
        for c in range(step):
            lanes = slice(c * LANES, (c + 1) * LANES)
            for g in range(0, groups, 2):
                two = [
                    block[c * rows : (c + 1) * rows, (g + n) * LANES : (g + n + 1) * LANES] for n in range(2)
                ]
                stacked[first // step, g * rows : (g + 2) * rows, lanes] = jnp.concatenate(two, axis=0).astype(BF16)
        turn = first // step % 2
        for c in range(step):
            part = proj_ref[(first + c) * narrow : (first + c + 1) * narrow, :]
            for m in range(members):
                start = c * LANES + m * narrow
                spread[turn, start : start + narrow, m * width : (m + 1) * width] = part
        term = matmul(stacked[first // step], spread[turn])
        total = term if total is None else total + term
    counts = matmul(left_mask_ref[...], right_ref[:, right_width:], TN)[:rows, :]
    scale = 1.0 / jnp.maximum(counts, 1.0)
    for m in range(members):
        for g in range(groups):
            j = m * groups + g
            part = total[g * rows : (g + 1) * rows, m * width : (m + 1) * width]
            moved[j * rows : (j + 1) * rows, :] = part * scale[:, j : j + 1]
    for i in range(rows):
        at = slice(i * cols, (i + 1) * cols)
        first = pair_ref[at, :].astype(F32) + moved[pl.ds(i, cols, stride=rows), :]
        first = first.astype(BF16)
        first_ref[at, :] = first
        normed_ref[at, :] = normalize(first.astype(F32)).astype(BF16)
    devices, pair, _ = tri_out_ref.shape
    half = devices * pair
    projections = matmul(tri_ref[...], normed_ref[...], NT)
    gated = jax.nn.sigmoid(projections[:half]) * projections[half:] * pair_mask_ref[...]
    gated = gated.astype(BF16)
    for d in range(devices):
        tri_out_ref[d] = gated[d * pair : (d + 1) * pair, :]


def triangle_kernel(row_count, col_count, rows, cols, own, given_ref, out_ref, opened, summed):
    residues = row_count * rows
    pair = 2 * own
    planes = opened.shape[0]
    each = -(-col_count // planes)

    def open_row(r, carry):
        for c in range(col_count):
            value = given_ref[r * col_count + c].astype(F32)
            lanes = slice(c % each * cols, (c % each + 1) * cols)
            for i in range(rows):
                start = pl.multiple_of((r * rows + i) * pair, pair)
                opened[c // each, pl.ds(start, pair), lanes] = value[:, i * cols : (i + 1) * cols]
        return carry

    lax.fori_loop(0, row_count, open_row, 0)
    used = each * cols
    for t in range(own):
        left = [opened.at[p][pl.ds(t, residues, stride=pair), :].astype(BF16) for p in range(planes)]
        right = [opened.at[p][pl.ds(own + t, residues, stride=pair), :].astype(BF16) for p in range(planes)]
        for q in range(planes):
            total = None
            for p in range(planes):
                width = min(each, col_count - p * each) * cols
                some = right[p][q * used : min((q + 1) * used, residues), :width]
                if some.shape[0] < LANES:
                    some = jnp.concatenate([some, jnp.zeros((LANES - some.shape[0], width), BF16)], axis=0)
                term = matmul(left[p][:, :width], some, NT)
                total = term if total is None else total + term
            summed.at[q][pl.ds(t, residues, stride=pair), :] = total

    def close_row(r, carry):
        for c in range(col_count):
            lanes = slice(c % each * cols, (c % each + 1) * cols)
            parts = []
            for i in range(rows):
                start = pl.multiple_of((r * rows + i) * pair, pair)
                parts.append(summed[c // each, pl.ds(start, pair), lanes])
            out_ref[r * col_count + c] = jnp.concatenate(parts, axis=1)[:own].astype(BF16)
        return carry

    lax.fori_loop(0, row_count, close_row, 0)


def partner(index, k, count):
    return index ^ k if count & (count - 1) == 0 else (index + k) % count


def source(index, k, count):
    return index ^ k if count & (count - 1) == 0 else lax.rem(index - k + count, count)


def triangle_by_channel(row_count, col_count, rows, cols, gated):
    devices, pair, places = gated.shape
    own = pair // 2
    gated = lax.all_to_all(gated, ("row", "col"), split_axis=0, concat_axis=0, tiled=True)
    residues = row_count * rows
    planes = -(-col_count // (LANES // cols))
    (summed,) = call(
        functools.partial(triangle_kernel, row_count, col_count, rows, cols, own),
        16,
        [((devices, own, places), BF16)],
        [pltpu.VMEM((planes, residues * pair, LANES), F32)] * 2,
    )(gated)
    summed = lax.all_to_all(summed, ("row", "col"), split_axis=0, concat_axis=0, tiled=True)
    return summed


def triangle_by_residue(row_count, col_count, rows, cols, gated):
    _, pair, places = gated.shape
    both = gated.reshape(2, pair // 2, rows, cols).transpose(0, 2, 3, 1)
    right = lax.all_gather(both[1], "row", axis=0, tiled=True)
    right = lax.all_to_all(right, "col", split_axis=0, concat_axis=1, tiled=True)
    left = lax.all_gather(both[0], "col", axis=1, tiled=True)
    summed = jnp.einsum("ikc,jkc->cij", left, right, preferred_element_type=F32)
    return summed.reshape(1, pair // 2, places).astype(BF16)


def gate_kernel(first_ref, normed_ref, gate_ref, first_t_ref, gated_ref):
    first_t_ref[...] = first_ref[...].astype(F32).T
    gated_ref[...] = jax.nn.sigmoid(matmul(gate_ref[...].T, normed_ref[...], NT))


def tail_kernel(first_ref, gated_ref, summed_ref, out_w_ref, in_ref, back_ref, out_ref, summed):
    own = summed_ref.shape[1]
    for d in range(summed_ref.shape[0]):
        summed[d * own : (d + 1) * own, :] = summed_ref[d].astype(F32)
    normed_sum = normalize(summed[...], 0).astype(BF16)
    update = gated_ref[...] * matmul(out_w_ref[...].T, normed_sum)
    second = (first_ref[...] + update).astype(BF16).astype(F32)
    normed_second = normalize(second, 0).astype(BF16)
    hidden = jnp.maximum(matmul(in_ref[...].T, normed_second), 0.0).astype(BF16)
    result = second + matmul(back_ref[...].T, hidden)
    out_ref[...] = result.T.astype(BF16)


def shards(
    row_count, col_count, alignment, alignment_mask, residue_mask, pair_features, outer_product_left, outer_product_right,
    outer_proj, triangle_proj, triangle_gate, triangle_out, transition_in, transition_out,
):
    rows, cols, width = pair_features.shape
    sequences, _, channels = alignment.shape
    narrow = outer_product_left.shape[1]
    inner = triangle_out.shape[0]
    devices = row_count * col_count
    turns = cols // rows
    places = rows * cols
    r, c = lax.axis_index("row"), lax.axis_index("col")
    by_channel = inner % devices == 0
    owners = devices if by_channel else 1
    own = inner // owners

    members = LANES // narrow
    right_lanes = cols * narrow + LANES
    left_lanes = rows * narrow + LANES
    lines = sequences * cols
    chunks = 4 if lines % 64 == 0 else 1
    pieces = 4 if narrow % 4 == 0 else 1

    hbm = pl.BlockSpec(memory_space=pltpu.HBM)
    right, left = call(
        functools.partial(side_kernel, chunks, narrow),
        16,
        [((row_count, sequences, right_lanes), BF16), ((turns, sequences, left_lanes), BF16)],
        [
            pltpu.VMEM((lines, LANES), F32),
            pltpu.VMEM((lines, LANES), F32),
            pltpu.VMEM((lines, channels), BF16),
            pltpu.VMEM((sequences, cols), jnp.int32),
            pltpu.VMEM((narrow, channels), BF16),
            pltpu.VMEM((narrow, channels), BF16),
            pltpu.VMEM((sequences, right_lanes), BF16),
            pltpu.SemaphoreType.DMA((chunks,)),
            pltpu.SemaphoreType.DMA,
            pltpu.SemaphoreType.DMA,
            pltpu.SemaphoreType.DMA,
            pltpu.SemaphoreType.DMA((row_count,)),
        ],
        [hbm] * 4,
        (hbm, VMEM),
    )(*in_hbm([alignment.reshape(lines, channels), alignment_mask, outer_product_left.T, outer_product_right.T]))
    right = lax.all_to_all(right, "row", split_axis=0, concat_axis=0, tiled=True)
    right = right.reshape(row_count * sequences, right_lanes)
    places_of = [(row, col) for row in range(row_count) for col in range(col_count)]

    def route(to):
        return [(row * col_count + col, to(row, col)[0] * col_count + to(row, col)[1]) for row, col in places_of]

    turned = route(lambda row, col: (turns * col + row % turns, row // turns))
    left = lax.ppermute(left, ("row", "col"), turned)
    lefts = []
    for d in range(turns):
        for k in range(col_count):
            near = route(
                lambda row, col: (row // turns * turns + (row + d) % turns, partner(col, k, col_count))
            )
            lefts.append(lax.ppermute(left[d], ("row", "col"), near) if d + k else left[0])

    residue_float = residue_mask.astype(F32)
    row_mask = lax.dynamic_slice_in_dim(residue_float, r * rows, rows)
    col_mask = lax.dynamic_slice_in_dim(residue_float, c * cols, cols)
    pair_mask = (row_mask[:, None] * col_mask[None, :]).reshape(1, places)
    tri_rows, left_t, left_mask = call(
        functools.partial(prepare_kernel, rows, narrow, turns, col_count, own),
        16,
        [
            ((4 * inner, width), BF16),
            ((rows * narrow, row_count * sequences), BF16),
            ((row_count * sequences, LANES), BF16),
        ],
        [pltpu.VMEM((row_count * sequences, left_lanes), BF16)],
    )(*in_hbm([triangle_proj] + lefts))

    first, normed_pair, gated = call(
        functools.partial(outer_kernel, rows, cols, narrow),
        24,
        [((places, width), BF16), ((places, width), BF16), ((owners, 2 * own, places), BF16)],
        [
            pltpu.VMEM((pieces, cols // members * rows, narrow // pieces * LANES), BF16),
            pltpu.VMEM((2, narrow // pieces * LANES, members * width), BF16),
            pltpu.VMEM((places, width), F32),
        ],
    )(left_t, left_mask, right, tri_rows, pair_mask, *in_hbm([pair_features.reshape(places, width), outer_proj]))

    first_t, gate = call(gate_kernel, 16, [((width, places), F32)] * 2, [])(first, normed_pair, triangle_gate)
    triangle = triangle_by_channel if by_channel else triangle_by_residue
    summed = triangle(row_count, col_count, rows, cols, gated)
    (out,) = call(tail_kernel, 16, [((places, width), BF16)], [pltpu.VMEM((inner, places), F32)])(
        first_t, gate, summed, triangle_out, transition_in, transition_out
    )
    return out.reshape(rows, cols, width)


def solution(mesh):
    placed = (
        P("row", "col", None),
        P("row", "col"),
        P(),
        P("row", "col", None),
    ) + (P(),) * 8

    def body(*args):
        return shards(mesh.shape["row"], mesh.shape["col"], *args)

    return jax.shard_map(body, mesh=mesh, in_specs=placed, out_specs=P("row", "col", None), check_vma=False)
```

```python
import functools

import jax
import jax.numpy as jnp
from jax import lax
from jax.experimental import pallas as pl
from jax.experimental.pallas import tpu as pltpu
from jax.sharding import PartitionSpec as P


epsilon = 1e-05
LANES = 128
BF16 = jnp.bfloat16
F32 = jnp.float32
NT = (((1,), (1,)), ((), ()))
TN = (((0,), (0,)), ((), ()))


def matmul(a, b, dims=(((1,), (0,)), ((), ()))):
    return lax.dot_general(a, b, dims, preferred_element_type=F32)


def iota(shape, axis):
    return lax.broadcasted_iota(jnp.int32, shape, axis)


def normalize(values, axis=-1):
    mean_value = jnp.mean(values, axis=axis, keepdims=True)
    centered = values - mean_value
    variance = jnp.mean(centered * centered, axis=axis, keepdims=True)
    return centered * lax.rsqrt(variance + epsilon)


def in_hbm(values):
    return [pltpu.with_memory_space_constraint(value, pltpu.HBM) for value in values]


def call(kernel, mebibytes, outs, scratch, in_specs=None, out_specs=None):
    return pl.pallas_call(
        kernel,
        out_shape=tuple(jax.ShapeDtypeStruct(*out) for out in outs),
        out_specs=out_specs or (VMEM,) * len(outs),
        scratch_shapes=scratch,
        compiler_params=pltpu.CompilerParams(vmem_limit_bytes=mebibytes * 1024 * 1024),
        **({} if in_specs is None else {"in_specs": in_specs}),
    )


VMEM = pl.BlockSpec(memory_space=pltpu.VMEM)


def pack_side(projected, mask, narrow, first, count, put):
    sequences, cols = mask.shape
    members = LANES // narrow
    lane = iota((sequences, LANES), 1)
    groups = count // members
    width = groups * LANES
    at = iota((cols, width), 1)
    residue = first + (at % LANES) // narrow * groups + at // LANES
    masks = matmul(mask, (iota((cols, width), 0) == residue).astype(BF16))
    for group in range(groups):
        value = None
        for member in range(members):
            part = projected[pl.ds(first + member * groups + group, sequences, stride=cols), :]
            value = part if value is None else jnp.where(lane >= member * narrow, part, value)
        put(group, (value * masks[:, group * LANES : (group + 1) * LANES]).astype(BF16))
    at = iota((cols, LANES), 1)
    pick = (iota((cols, LANES), 0) - first == at) & (at < count)
    put(groups, matmul(mask, pick.astype(BF16)).astype(BF16))


def side_kernel(
    chunks, narrow, align_hbm, mask_hbm, left_w_hbm, right_w_hbm, right_hbm, left_ref,
    left_rows, right_rows, align, mask_int, left_w, right_w, packed, align_sem, mask_sem, left_sem, right_sem, out_sem,
):
    chunk = align.shape[0] // chunks
    small = [
        pltpu.make_async_copy(left_w_hbm, left_w, left_sem),
        pltpu.make_async_copy(right_w_hbm, right_w, right_sem),
        pltpu.make_async_copy(mask_hbm, mask_int, mask_sem),
    ]
    parts = []
    for n in range(chunks):
        at = pl.ds(n * chunk, chunk)
        parts.append(pltpu.make_async_copy(align_hbm.at[at, :], align.at[at, :], align_sem.at[n]))
    for copy in small[:2] + parts + small[2:]:
        copy.start()
    small[0].wait()
    small[1].wait()
    members = LANES // narrow
    both = jnp.concatenate([left_w[...]] * members + [right_w[...]] * members, axis=0)
    for n in range(chunks):
        parts[n].wait()
        at = slice(n * chunk, (n + 1) * chunk)
        normed = normalize(align[at, :].astype(F32)).astype(BF16)
        value = matmul(normed, both, NT)
        left_rows[at, :] = value[:, :LANES]
        right_rows[at, :] = value[:, LANES:]
    small[2].wait()
    mask = mask_int[...].astype(BF16)
    cols = mask.shape[1]

    def put_right(group, value):
        packed[:, group * LANES : (group + 1) * LANES] = value

    pack_side(right_rows, mask, narrow, 0, cols, put_right)
    copies = [pltpu.make_async_copy(packed, right_hbm.at[n], out_sem.at[n]) for n in range(right_hbm.shape[0])]
    for copy in copies:
        copy.start()
    turns = left_ref.shape[0]
    turn = lax.rem(lax.axis_index("row"), turns)
    for h in range(turns):
        place = lax.rem(h - turn + turns, turns)

        def put_left(group, value):
            left_ref[place, :, group * LANES : (group + 1) * LANES] = value

        pack_side(left_rows, mask, narrow, h * (cols // turns), cols // turns, put_left)
    for copy in copies:
        copy.wait()


def prepare_kernel(rows, narrow, turns, sources, own, tri_ref, *refs):
    left_refs, refs = refs[: turns * sources], refs[turns * sources :]
    tri_rows_ref, left_t_ref, mask_ref, gathered = refs
    block = left_refs[0].shape[0]
    h, column = lax.rem(lax.axis_index("row"), turns), lax.axis_index("col")
    for n, left_ref in enumerate(left_refs):
        d, k = n // sources, n % sources
        start = (source(column, k, sources) * turns + lax.rem(h - d + turns, turns)) * block
        gathered[pl.ds(pl.multiple_of(start, block), block), :] = left_ref[...]
    out = tri_ref.shape[0]
    members = LANES // narrow
    width = rows * narrow
    groups = rows // members
    at = iota((width, width), 0)
    channel, residue = at // rows, at % rows
    place = residue % groups * LANES + residue // groups * narrow + channel
    pick = (iota((width, width), 1) == place).astype(BF16)
    left_t_ref[...] = matmul(pick, gathered[:, :width], NT).astype(BF16)
    mask_ref[...] = gathered[:, width:]
    at = iota((4 * out, 4 * out), 0)
    kind, rest = at // (2 * out), at % (2 * out)
    owner, side, channel = rest // (2 * own), rest // own % 2, rest % own
    column = side * 2 * out + kind * out + owner * own + channel
    pick = (iota((4 * out, 4 * out), 1) == column).astype(BF16)
    tri_rows_ref[...] = matmul(pick, tri_ref[...], NT).astype(BF16)


def outer_kernel(
    rows, cols, narrow, left_t, left_mask_ref, right_ref, tri_ref, pair_mask_ref, pair_ref, proj_ref,
    first_ref, normed_ref, tri_out_ref, stacked, spread, moved,
):
    members = LANES // narrow
    groups = cols // members
    right_width = cols * narrow
    width = pair_ref.shape[1]
    steps = stacked.shape[0]
    step = narrow // steps
    spread[...] = jnp.zeros_like(spread)
    total = None
    for first in range(0, narrow, step):
        block = matmul(left_t[first * rows : (first + step) * rows, :], right_ref[:, :right_width])
        for c in range(step):
            lanes = slice(c * LANES, (c + 1) * LANES)
            for g in range(0, groups, 2):
                two = [
                    block[c * rows : (c + 1) * rows, (g + n) * LANES : (g + n + 1) * LANES] for n in range(2)
                ]
                stacked[first // step, g * rows : (g + 2) * rows, lanes] = jnp.concatenate(two, axis=0).astype(BF16)
        turn = first // step % 2
        for c in range(step):
            part = proj_ref[(first + c) * narrow : (first + c + 1) * narrow, :]
            for m in range(members):
                start = c * LANES + m * narrow
                spread[turn, start : start + narrow, m * width : (m + 1) * width] = part
        term = matmul(stacked[first // step], spread[turn])
        total = term if total is None else total + term
    counts = matmul(left_mask_ref[...], right_ref[:, right_width:], TN)[:rows, :]
    scale = 1.0 / jnp.maximum(counts, 1.0)
    for m in range(members):
        for g in range(groups):
            j = m * groups + g
            part = total[g * rows : (g + 1) * rows, m * width : (m + 1) * width]
            moved[j * rows : (j + 1) * rows, :] = part * scale[:, j : j + 1]
    for i in range(rows):
        at = slice(i * cols, (i + 1) * cols)
        first = pair_ref[at, :].astype(F32) + moved[pl.ds(i, cols, stride=rows), :]
        first = first.astype(BF16)
        first_ref[at, :] = first
        normed_ref[at, :] = normalize(first.astype(F32)).astype(BF16)
    devices, pair, _ = tri_out_ref.shape
    half = devices * pair
    projections = matmul(tri_ref[...], normed_ref[...], NT)
    gated = jax.nn.sigmoid(projections[:half]) * projections[half:] * pair_mask_ref[...]
    gated = gated.astype(BF16)
    for d in range(devices):
        tri_out_ref[d] = gated[d * pair : (d + 1) * pair, :]


def triangle_kernel(row_count, col_count, rows, cols, own, given_ref, out_ref, opened, summed):
    residues = row_count * rows
    pair = 2 * own
    planes = opened.shape[0]
    each = -(-col_count // planes)

    def open_row(r, carry):
        for c in range(col_count):
            value = given_ref[r * col_count + c].astype(F32)
            lanes = slice(c % each * cols, (c % each + 1) * cols)
            for i in range(rows):
                start = pl.multiple_of((r * rows + i) * pair, pair)
                opened[c // each, pl.ds(start, pair), lanes] = value[:, i * cols : (i + 1) * cols]
        return carry

    lax.fori_loop(0, row_count, open_row, 0)
    used = each * cols
    for t in range(own):
        left = [opened.at[p][pl.ds(t, residues, stride=pair), :].astype(BF16) for p in range(planes)]
        right = [opened.at[p][pl.ds(own + t, residues, stride=pair), :].astype(BF16) for p in range(planes)]
        for q in range(planes):
            total = None
            for p in range(planes):
                width = min(each, col_count - p * each) * cols
                some = right[p][q * used : min((q + 1) * used, residues), :width]
                if some.shape[0] < LANES:
                    some = jnp.concatenate([some, jnp.zeros((LANES - some.shape[0], width), BF16)], axis=0)
                term = matmul(left[p][:, :width], some, NT)
                total = term if total is None else total + term
            summed.at[q][pl.ds(t, residues, stride=pair), :] = total

    def close_row(r, carry):
        for c in range(col_count):
            lanes = slice(c % each * cols, (c % each + 1) * cols)
            parts = []
            for i in range(rows):
                start = pl.multiple_of((r * rows + i) * pair, pair)
                parts.append(summed[c // each, pl.ds(start, pair), lanes])
            out_ref[r * col_count + c] = jnp.concatenate(parts, axis=1)[:own].astype(BF16)
        return carry

    lax.fori_loop(0, row_count, close_row, 0)


def partner(index, k, count):
    return index ^ k if count & (count - 1) == 0 else (index + k) % count


def source(index, k, count):
    return index ^ k if count & (count - 1) == 0 else lax.rem(index - k + count, count)


def triangle_by_channel(row_count, col_count, rows, cols, gated):
    devices, pair, places = gated.shape
    own = pair // 2
    gated = lax.all_to_all(gated, ("row", "col"), split_axis=0, concat_axis=0, tiled=True)
    residues = row_count * rows
    planes = -(-col_count // (LANES // cols))
    (summed,) = call(
        functools.partial(triangle_kernel, row_count, col_count, rows, cols, own),
        16,
        [((devices, own, places), BF16)],
        [pltpu.VMEM((planes, residues * pair, LANES), F32)] * 2,
    )(gated)
    summed = lax.all_to_all(summed, ("row", "col"), split_axis=0, concat_axis=0, tiled=True)
    return summed


def triangle_by_residue(row_count, col_count, rows, cols, gated):
    _, pair, places = gated.shape
    both = gated.reshape(2, pair // 2, rows, cols).transpose(0, 2, 3, 1)
    right = lax.all_gather(both[1], "row", axis=0, tiled=True)
    right = lax.all_to_all(right, "col", split_axis=0, concat_axis=1, tiled=True)
    left = lax.all_gather(both[0], "col", axis=1, tiled=True)
    summed = jnp.einsum("ikc,jkc->cij", left, right, preferred_element_type=F32)
    return summed.reshape(1, pair // 2, places).astype(BF16)


def gate_kernel(first_ref, normed_ref, gate_ref, first_t_ref, gated_ref):
    first_t_ref[...] = first_ref[...].astype(F32).T
    gated_ref[...] = jax.nn.sigmoid(matmul(gate_ref[...].T, normed_ref[...], NT))


def tail_kernel(first_ref, gated_ref, summed_ref, out_w_ref, in_ref, back_ref, out_ref, summed):
    own = summed_ref.shape[1]
    for d in range(summed_ref.shape[0]):
        summed[d * own : (d + 1) * own, :] = summed_ref[d].astype(F32)
    normed_sum = normalize(summed[...], 0).astype(BF16)
    update = gated_ref[...] * matmul(out_w_ref[...].T, normed_sum)
    second = (first_ref[...] + update).astype(BF16).astype(F32)
    normed_second = normalize(second, 0).astype(BF16)
    hidden = jnp.maximum(matmul(in_ref[...].T, normed_second), 0.0).astype(BF16)
    result = second + matmul(back_ref[...].T, hidden)
    out_ref[...] = result.T.astype(BF16)


def shards(
    row_count, col_count, alignment, alignment_mask, residue_mask, pair_features, outer_product_left, outer_product_right,
    outer_proj, triangle_proj, triangle_gate, triangle_out, transition_in, transition_out,
):
    rows, cols, width = pair_features.shape
    sequences, _, channels = alignment.shape
    narrow = outer_product_left.shape[1]
    inner = triangle_out.shape[0]
    devices = row_count * col_count
    turns = cols // rows
    places = rows * cols
    r, c = lax.axis_index("row"), lax.axis_index("col")
    by_channel = inner % devices == 0
    owners = devices if by_channel else 1
    own = inner // owners

    members = LANES // narrow
    right_lanes = cols * narrow + LANES
    left_lanes = rows * narrow + LANES
    lines = sequences * cols
    chunks = 1
    pieces = 4 if narrow % 4 == 0 else 1

    hbm = pl.BlockSpec(memory_space=pltpu.HBM)
    right, left = call(
        functools.partial(side_kernel, chunks, narrow),
        16,
        [((row_count, sequences, right_lanes), BF16), ((turns, sequences, left_lanes), BF16)],
        [
            pltpu.VMEM((lines, LANES), F32),
            pltpu.VMEM((lines, LANES), F32),
            pltpu.VMEM((lines, channels), BF16),
            pltpu.VMEM((sequences, cols), jnp.int32),
            pltpu.VMEM((narrow, channels), BF16),
            pltpu.VMEM((narrow, channels), BF16),
            pltpu.VMEM((sequences, right_lanes), BF16),
            pltpu.SemaphoreType.DMA((chunks,)),
            pltpu.SemaphoreType.DMA,
            pltpu.SemaphoreType.DMA,
            pltpu.SemaphoreType.DMA,
            pltpu.SemaphoreType.DMA((row_count,)),
        ],
        [hbm] * 4,
        (hbm, VMEM),
    )(*in_hbm([alignment.reshape(lines, channels), alignment_mask, outer_product_left.T, outer_product_right.T]))
    right = lax.all_to_all(right, "row", split_axis=0, concat_axis=0, tiled=True)
    right = right.reshape(row_count * sequences, right_lanes)
    places_of = [(row, col) for row in range(row_count) for col in range(col_count)]

    def route(to):
        return [(row * col_count + col, to(row, col)[0] * col_count + to(row, col)[1]) for row, col in places_of]

    turned = route(lambda row, col: (turns * col + row % turns, row // turns))
    left = lax.ppermute(left, ("row", "col"), turned)
    lefts = []
    for d in range(turns):
        for k in range(col_count):
            near = route(
                lambda row, col: (row // turns * turns + (row + d) % turns, partner(col, k, col_count))
            )
            lefts.append(lax.ppermute(left[d], ("row", "col"), near) if d + k else left[0])

    residue_float = residue_mask.astype(F32)
    row_mask = lax.dynamic_slice_in_dim(residue_float, r * rows, rows)
    col_mask = lax.dynamic_slice_in_dim(residue_float, c * cols, cols)
    pair_mask = (row_mask[:, None] * col_mask[None, :]).reshape(1, places)
    tri_rows, left_t, left_mask = call(
        functools.partial(prepare_kernel, rows, narrow, turns, col_count, own),
        16,
        [
            ((4 * inner, width), BF16),
            ((rows * narrow, row_count * sequences), BF16),
            ((row_count * sequences, LANES), BF16),
        ],
        [pltpu.VMEM((row_count * sequences, left_lanes), BF16)],
    )(triangle_proj, *lefts)

    first, normed_pair, gated = call(
        functools.partial(outer_kernel, rows, cols, narrow),
        24,
        [((places, width), BF16), ((places, width), BF16), ((owners, 2 * own, places), BF16)],
        [
            pltpu.VMEM((pieces, cols // members * rows, narrow // pieces * LANES), BF16),
            pltpu.VMEM((2, narrow // pieces * LANES, members * width), BF16),
            pltpu.VMEM((places, width), F32),
        ],
    )(left_t, left_mask, right, tri_rows, pair_mask, pair_features.reshape(places, width), outer_proj)

    first_t, gate = call(gate_kernel, 16, [((width, places), F32)] * 2, [])(first, normed_pair, triangle_gate)
    triangle = triangle_by_channel if by_channel else triangle_by_residue
    summed = triangle(row_count, col_count, rows, cols, gated)
    (out,) = call(tail_kernel, 16, [((places, width), BF16)], [pltpu.VMEM((inner, places), F32)])(
        first_t, gate, summed, triangle_out, transition_in, transition_out
    )
    return out.reshape(rows, cols, width)


def solution(mesh):
    placed = (
        P("row", "col", None),
        P("row", "col"),
        P(),
        P("row", "col", None),
    ) + (P(),) * 8

    def body(*args):
        return shards(mesh.shape["row"], mesh.shape["col"], *args)

    return jax.shard_map(body, mesh=mesh, in_specs=placed, out_specs=P("row", "col", None), check_vma=False)
```

```python
import functools

import jax
import jax.numpy as jnp
from jax import lax
from jax.experimental import pallas as pl
from jax.experimental.pallas import tpu as pltpu
from jax.sharding import PartitionSpec as P


epsilon = 1e-05
LANES = 128
BF16 = jnp.bfloat16
F32 = jnp.float32
NT = (((1,), (1,)), ((), ()))
TN = (((0,), (0,)), ((), ()))


def matmul(a, b, dims=(((1,), (0,)), ((), ()))):
    return lax.dot_general(a, b, dims, preferred_element_type=F32)


def iota(shape, axis):
    return lax.broadcasted_iota(jnp.int32, shape, axis)


def normalize(values, axis=-1):
    mean_value = jnp.mean(values, axis=axis, keepdims=True)
    centered = values - mean_value
    variance = jnp.mean(centered * centered, axis=axis, keepdims=True)
    return centered * lax.rsqrt(variance + epsilon)


def in_hbm(values):
    return [pltpu.with_memory_space_constraint(value, pltpu.HBM) for value in values]


def call(kernel, mebibytes, outs, scratch, in_specs=None, out_specs=None):
    return pl.pallas_call(
        kernel,
        out_shape=tuple(jax.ShapeDtypeStruct(*out) for out in outs),
        out_specs=out_specs or (VMEM,) * len(outs),
        scratch_shapes=scratch,
        compiler_params=pltpu.CompilerParams(vmem_limit_bytes=mebibytes * 1024 * 1024),
        **({} if in_specs is None else {"in_specs": in_specs}),
    )


VMEM = pl.BlockSpec(memory_space=pltpu.VMEM)


def pack_side(projected, mask, narrow, first, count, put):
    sequences, cols = mask.shape
    members = LANES // narrow
    lane = iota((sequences, LANES), 1)
    groups = count // members
    width = groups * LANES
    residue = first + iota((cols, width), 1) // narrow
    masks = matmul(mask, (iota((cols, width), 0) == residue).astype(BF16))
    for group in range(groups):
        value = None
        for member in range(members):
            part = projected[pl.ds(first + group * members + member, sequences, stride=cols), :]
            value = part if value is None else jnp.where(lane >= member * narrow, part, value)
        put(group, (value * masks[:, group * LANES : (group + 1) * LANES]).astype(BF16))
    at = iota((cols, LANES), 1)
    pick = (iota((cols, LANES), 0) - first == at) & (at < count)
    put(groups, matmul(mask, pick.astype(BF16)).astype(BF16))


def side_kernel(
    narrow, align_hbm, mask_hbm, left_w_hbm, right_w_hbm, right_hbm, left_ref,
    left_rows, right_rows, align, mask_int, left_w, right_w, packed, align_sem, mask_sem, left_sem, right_sem, out_sem,
):
    fetches = [
        pltpu.make_async_copy(left_w_hbm, left_w, left_sem),
        pltpu.make_async_copy(right_w_hbm, right_w, right_sem),
        pltpu.make_async_copy(align_hbm, align, align_sem),
        pltpu.make_async_copy(mask_hbm, mask_int, mask_sem),
    ]
    for copy in fetches:
        copy.start()
    for copy in fetches:
        copy.wait()
    members = LANES // narrow
    both = jnp.concatenate([left_w[...]] * members + [right_w[...]] * members, axis=0)
    normed = normalize(align[...].astype(F32)).astype(BF16)
    value = matmul(normed, both, NT)
    left_rows[...] = value[:, :LANES]
    right_rows[...] = value[:, LANES:]
    mask = mask_int[...].astype(BF16)
    cols = mask.shape[1]
    parts = packed.shape[0]
    for h in range(parts):

        def put_right(group, value):
            packed[h, :, group * LANES : (group + 1) * LANES] = value

        pack_side(right_rows, mask, narrow, h * (cols // parts), cols // parts, put_right)
    copies = [
        pltpu.make_async_copy(packed.at[n % parts], right_hbm.at[n], out_sem.at[n])
        for n in range(right_hbm.shape[0])
    ]
    for copy in copies:
        copy.start()

    def put_left(group, value):
        left_ref[:, group * LANES : (group + 1) * LANES] = value

    pack_side(left_rows, mask, narrow, 0, cols, put_left)
    for copy in copies:
        copy.wait()


def prepare_kernel(own, tri_ref, pair_ref, *refs):
    *given_refs, block_ref, tri_rows_ref = refs
    rows, cols, _ = pair_ref.shape
    parts = cols // rows
    x = lax.rem(lax.axis_index("row"), parts)
    for i in range(rows):
        at = pl.ds(pl.multiple_of((x * rows + i) * rows, 8), rows)
        block_ref[at, :] = pair_ref[i, pl.ds(pl.multiple_of(x * rows, 8), rows), :]
        for d, given_ref in enumerate(given_refs, 1):
            at = pl.ds(pl.multiple_of((lax.rem(x - d + parts, parts) * rows + i) * rows, 8), rows)
            block_ref[at, :] = given_ref[i]
    out = tri_ref.shape[0]
    at = iota((4 * out, 4 * out), 0)
    kind, rest = at // (2 * out), at % (2 * out)
    owner, side, channel = rest // (2 * own), rest // own % 2, rest % own
    column = side * 2 * out + kind * out + owner * own + channel
    pick = (iota((4 * out, 4 * out), 1) == column).astype(BF16)
    tri_rows_ref[...] = matmul(pick, tri_ref[...], NT).astype(BF16)


def outer_kernel(tall, short, narrow, parts, right_ref, pair_ref, proj_ref, tri_ref, pair_mask_ref, *refs):
    *left_refs, first_ref, tri_out_ref, left, right_t, proj, stacked, spread, moved, normed = refs
    sources = len(left_refs) // parts
    sequences = left_refs[0].shape[0]
    x, column = lax.rem(lax.axis_index("row"), parts), lax.axis_index("col")
    for n, left_ref in enumerate(left_refs):
        d, k = n // sources, n % sources
        start = (source(column, k, sources) * parts + lax.rem(x - d + parts, parts)) * sequences
        left[pl.ds(pl.multiple_of(start, sequences), sequences), :] = left_ref[...]
    members = LANES // narrow
    groups = tall // members
    left_width, right_width = tall * narrow, short * narrow
    width = pair_ref.shape[1]
    planes = right_t.shape[0]
    for p in range(planes):
        right_t[p] = right_ref[p * LANES : (p + 1) * LANES, :right_width].astype(F32).T
    proj[...] = proj_ref[...].astype(F32)
    steps = stacked.shape[0]
    step = narrow // steps
    spread[...] = jnp.zeros_like(spread)
    total = None
    for n in range(steps):
        some = []
        for p in range(planes):
            each = [right_t.at[p][pl.ds(n * step + d, short, stride=narrow), :] for d in range(step)]
            some.append(jnp.concatenate(each, axis=0).astype(BF16))
        block = matmul(jnp.concatenate(some, axis=1), left[:, :left_width])
        for d in range(step):
            lanes = slice(d * LANES, (d + 1) * LANES)
            for g in range(0, groups, 2):
                two = [
                    block[d * short : (d + 1) * short, (g + m) * LANES : (g + m + 1) * LANES] for m in range(2)
                ]
                stacked[n, g * short : (g + 2) * short, lanes] = jnp.concatenate(two, axis=0).astype(BF16)
            part = proj[pl.ds(n * step + d, narrow, stride=narrow), :].astype(BF16)
            for m in range(members):
                start = d * LANES + m * narrow
                spread[n % 2, start : start + narrow, m * width : (m + 1) * width] = part
        term = matmul(stacked[n], spread[n % 2])
        total = term if total is None else total + term
    counts = matmul(right_ref[:, right_width:], left[:, left_width:], TN)[:short, :]
    scale = 1.0 / jnp.maximum(counts, 1.0)
    for g in range(groups):
        for m in range(members):
            i = g * members + m
            at = slice(i * short, (i + 1) * short)
            part = total[g * short : (g + 1) * short, m * width : (m + 1) * width]
            moved[at, :] = part * scale[:, i : i + 1] + pair_ref[at, :].astype(F32)
    for j in range(short):
        first = moved[pl.ds(j, tall, stride=short), :].astype(BF16)
        first_ref[j * tall : (j + 1) * tall, :] = first
        normed[j * tall : (j + 1) * tall, :] = normalize(first.astype(F32)).astype(BF16)
    devices, pair, _ = tri_out_ref.shape
    half = devices * pair
    projections = matmul(tri_ref[...], normed[...], NT)
    gated = jax.nn.sigmoid(projections[:half]) * projections[half:] * pair_mask_ref[...]
    gated = gated.astype(BF16)
    for d in range(devices):
        tri_out_ref[d] = gated[d * pair : (d + 1) * pair, :]


def triangle_kernel(row_count, col_count, rows, cols, own, given_ref, out_ref, opened, summed):
    pair = 2 * own
    planes = opened.shape[0]
    parts = cols // rows
    each = -(-col_count // planes)
    used = each * cols

    def open_column(c, carry):
        for a in range(col_count):
            lanes = slice(a % each * cols, (a % each + 1) * cols)
            for x in range(parts):
                value = given_ref[(a * parts + x) * col_count + c].astype(F32)
                for k in range(rows):
                    start = pl.multiple_of((c * cols + x * rows + k) * pair, pair)
                    opened[a // each, pl.ds(start, pair), lanes] = value[:, k * cols : (k + 1) * cols]
        return carry

    residues = row_count * rows
    lax.fori_loop(0, col_count, open_column, 0)
    for t in range(own):
        left = [opened.at[p][pl.ds(t, residues, stride=pair), :].astype(BF16) for p in range(planes)]
        right = [opened.at[p][pl.ds(own + t, residues, stride=pair), :].astype(BF16) for p in range(planes)]
        for p in range(planes):
            count = min(used, residues - p * used)
            for q in range(planes):
                total = matmul(left[p], right[q], TN)[:count]
                summed.at[q][pl.ds(p * used * pair + t, count, stride=pair), :] = total

    def close_row(r, carry):
        for c in range(col_count):
            lanes = slice(c % each * cols, (c % each + 1) * cols)
            parts = []
            for i in range(rows):
                start = pl.multiple_of((r * rows + i) * pair, pair)
                parts.append(summed[c // each, pl.ds(start, pair), lanes])
            out_ref[r * col_count + c] = jnp.concatenate(parts, axis=1)[:own].astype(BF16)
        return carry

    lax.fori_loop(0, row_count, close_row, 0)


def partner(index, k, count):
    return index ^ k if count & (count - 1) == 0 else (index + k) % count


def source(index, k, count):
    return index ^ k if count & (count - 1) == 0 else lax.rem(index - k + count, count)


def triangle_by_channel(row_count, col_count, rows, cols, gated):
    devices, pair, places = gated.shape
    own = pair // 2
    gated = lax.all_to_all(gated, ("row", "col"), split_axis=0, concat_axis=0, tiled=True)
    residues = row_count * rows
    planes = -(-col_count // (LANES // cols))
    (summed,) = call(
        functools.partial(triangle_kernel, row_count, col_count, rows, cols, own),
        16,
        [((devices, own, places), BF16)],
        [pltpu.VMEM((planes, residues * pair, LANES), F32)] * 2,
    )(gated)
    summed = lax.all_to_all(summed, ("row", "col"), split_axis=0, concat_axis=0, tiled=True)
    return summed


def triangle_by_residue(row_count, col_count, rows, cols, gated):
    _, pair, places = gated.shape
    both = gated.reshape(2, pair // 2, cols, rows).transpose(0, 3, 2, 1)
    right = lax.all_gather(both[1], "row", axis=0, tiled=True)
    right = lax.all_to_all(right, "col", split_axis=0, concat_axis=1, tiled=True)
    left = lax.all_gather(both[0], "col", axis=1, tiled=True)
    summed = jnp.einsum("ikc,jkc->cij", left, right, preferred_element_type=F32)
    return summed.reshape(1, pair // 2, places).astype(BF16)


def gate_kernel(first_ref, gate_w_ref, *refs):
    *given_refs, first_t_ref, gated_ref, home = refs
    rows, cols, _ = first_ref.shape
    parts = cols // rows
    x = lax.rem(lax.axis_index("row"), parts)
    for j in range(rows):
        value = first_ref[j, pl.ds(pl.multiple_of(x * rows, 8), rows), :]
        home[pl.ds(x * rows + j, rows, stride=cols), :] = value.astype(F32)
        for d, given_ref in enumerate(given_refs, 1):
            at = pl.ds(lax.rem(x - d + parts, parts) * rows + j, rows, stride=cols)
            home[at, :] = given_ref[j].astype(F32)
    first = home[...]
    first_t_ref[...] = first.T
    gated_ref[...] = jax.nn.sigmoid(matmul(gate_w_ref[...].T, normalize(first).astype(BF16), NT))


def tail_kernel(first_ref, gated_ref, summed_ref, out_w_ref, in_ref, back_ref, out_ref, summed):
    own = summed_ref.shape[1]
    for d in range(summed_ref.shape[0]):
        summed[d * own : (d + 1) * own, :] = summed_ref[d].astype(F32)
    normed_sum = normalize(summed[...], 0).astype(BF16)
    update = gated_ref[...] * matmul(out_w_ref[...].T, normed_sum)
    second = (first_ref[...] + update).astype(BF16).astype(F32)
    normed_second = normalize(second, 0).astype(BF16)
    hidden = jnp.maximum(matmul(in_ref[...].T, normed_second), 0.0).astype(BF16)
    result = second + matmul(back_ref[...].T, hidden)
    out_ref[...] = result.T.astype(BF16)


def shards(
    row_count, col_count, alignment, alignment_mask, residue_mask, pair_features, outer_product_left, outer_product_right,
    outer_proj, triangle_proj, triangle_gate, triangle_out, transition_in, transition_out,
):
    rows, cols, width = pair_features.shape
    sequences, _, channels = alignment.shape
    narrow = outer_product_left.shape[1]
    inner = triangle_out.shape[0]
    devices = row_count * col_count
    turns = cols // rows
    places = rows * cols
    r, c = lax.axis_index("row"), lax.axis_index("col")
    by_channel = inner % devices == 0
    owners = devices if by_channel else 1
    own = inner // owners
    members = LANES // narrow
    right_lanes = rows * narrow + LANES
    left_lanes = cols * narrow + LANES
    lines = sequences * cols
    pieces = 4 if narrow % 4 == 0 else 1
    x = r % turns

    hbm = pl.BlockSpec(memory_space=pltpu.HBM)
    right, left = call(
        functools.partial(side_kernel, narrow),
        16,
        [((row_count, sequences, right_lanes), BF16), ((sequences, left_lanes), BF16)],
        [
            pltpu.VMEM((lines, LANES), F32),
            pltpu.VMEM((lines, LANES), F32),
            pltpu.VMEM((lines, channels), BF16),
            pltpu.VMEM((sequences, cols), jnp.int32),
            pltpu.VMEM((narrow, channels), BF16),
            pltpu.VMEM((narrow, channels), BF16),
            pltpu.VMEM((turns, sequences, right_lanes), BF16),
            pltpu.SemaphoreType.DMA,
            pltpu.SemaphoreType.DMA,
            pltpu.SemaphoreType.DMA,
            pltpu.SemaphoreType.DMA,
            pltpu.SemaphoreType.DMA((row_count,)),
        ],
        [hbm] * 4,
        (hbm, VMEM),
    )(*in_hbm([alignment.reshape(lines, channels), alignment_mask, outer_product_left.T, outer_product_right.T]))
    right = lax.all_to_all(right, "row", split_axis=0, concat_axis=0, tiled=True)
    right = right.reshape(row_count * sequences, right_lanes)
    places_of = [(row, col) for row in range(row_count) for col in range(col_count)]

    def route(to):
        return [(row * col_count + col, to(row, col)[0] * col_count + to(row, col)[1]) for row, col in places_of]

    def near(d, k):
        return route(lambda row, col: (row // turns * turns + (row + d) % turns, partner(col, k, col_count)))

    def exchange(values):
        given = []
        for d in range(1, turns):
            part = lax.dynamic_slice_in_dim(values, (x + d) % turns * rows, rows, 1)
            given.append(lax.ppermute(part, ("row", "col"), near(d, 0)))
        return given

    turned = route(lambda row, col: (turns * col + row % turns, row // turns))
    left = lax.ppermute(left, ("row", "col"), turned)
    across = [left] + [lax.ppermute(left, ("row", "col"), near(d, 0)) for d in range(1, turns)]
    blocks = {(d, 0): value for d, value in enumerate(across)}
    if col_count & (col_count - 1) == 0:
        bit = col_count // 2
        while bit:
            for d, k in list(blocks):
                blocks[d, k | bit] = lax.ppermute(blocks[d, k], ("row", "col"), near(0, bit))
            bit //= 2
    else:
        for d in range(turns):
            for k in range(1, col_count):
                blocks[d, k] = lax.ppermute(across[d], ("row", "col"), near(0, k))
    lefts = [blocks[d, k] for d in range(turns) for k in range(col_count)]
    pairs = exchange(pair_features)

    residue_float = residue_mask.astype(F32)
    row_mask = lax.dynamic_slice_in_dim(residue_float, r // turns * cols, cols)
    col_mask = lax.dynamic_slice_in_dim(residue_float, c * cols + x * rows, rows)
    pair_mask = (col_mask[:, None] * row_mask[None, :]).reshape(1, places)
    block, tri_rows = call(
        functools.partial(prepare_kernel, own), 16, [((places, width), BF16), ((4 * inner, width), BF16)], []
    )(triangle_proj, pair_features, *pairs)

    first, gated = call(
        functools.partial(outer_kernel, cols, rows, narrow, turns),
        24,
        [((places, width), BF16), ((owners, 2 * own, places), BF16)],
        [
            pltpu.VMEM((row_count * sequences, left_lanes), BF16),
            pltpu.VMEM((row_count * sequences // LANES, rows * narrow, LANES), F32),
            pltpu.VMEM((narrow * narrow, width), F32),
            pltpu.VMEM((pieces, cols // members * rows, narrow // pieces * LANES), BF16),
            pltpu.VMEM((2, narrow // pieces * LANES, members * width), BF16),
            pltpu.VMEM((places, width), F32),
            pltpu.VMEM((places, width), BF16),
        ],
    )(right, block, outer_proj, tri_rows, pair_mask, *lefts)

    first = first.reshape(rows, cols, width)
    firsts = exchange(first)
    first_t, gate = call(gate_kernel, 16, [((width, places), F32)] * 2, [pltpu.VMEM((places, width), F32)])(
        first, triangle_gate, *firsts
    )
    triangle = triangle_by_channel if by_channel else triangle_by_residue
    summed = triangle(row_count, col_count, rows, cols, gated)
    (out,) = call(tail_kernel, 16, [((places, width), BF16)], [pltpu.VMEM((inner, places), F32)])(
        first_t, gate, summed, triangle_out, transition_in, transition_out
    )
    return out.reshape(rows, cols, width)


def solution(mesh):
    placed = (
        P("row", "col", None),
        P("row", "col"),
        P(),
        P("row", "col", None),
    ) + (P(),) * 8

    def body(*args):
        return shards(mesh.shape["row"], mesh.shape["col"], *args)

    return jax.shard_map(body, mesh=mesh, in_specs=placed, out_specs=P("row", "col", None), check_vma=False)
```

```python
import functools

import jax
import jax.numpy as jnp
from jax import lax
from jax.experimental import pallas as pl
from jax.experimental.pallas import tpu as pltpu
from jax.sharding import PartitionSpec as P


epsilon = 1e-05
LANES = 128
BF16 = jnp.bfloat16
F32 = jnp.float32
NT = (((1,), (1,)), ((), ()))
TN = (((0,), (0,)), ((), ()))


def matmul(a, b, dims=(((1,), (0,)), ((), ()))):
    return lax.dot_general(a, b, dims, preferred_element_type=F32)


def iota(shape, axis):
    return lax.broadcasted_iota(jnp.int32, shape, axis)


def normalize(values, axis=-1):
    mean_value = jnp.mean(values, axis=axis, keepdims=True)
    centered = values - mean_value
    variance = jnp.mean(centered * centered, axis=axis, keepdims=True)
    return centered * lax.rsqrt(variance + epsilon)


def in_hbm(values):
    return [pltpu.with_memory_space_constraint(value, pltpu.HBM) for value in values]


def call(kernel, mebibytes, outs, scratch, in_specs=None, out_specs=None):
    return pl.pallas_call(
        kernel,
        out_shape=tuple(jax.ShapeDtypeStruct(*out) for out in outs),
        out_specs=out_specs or (VMEM,) * len(outs),
        scratch_shapes=scratch,
        compiler_params=pltpu.CompilerParams(vmem_limit_bytes=mebibytes * 1024 * 1024),
        **({} if in_specs is None else {"in_specs": in_specs}),
    )


VMEM = pl.BlockSpec(memory_space=pltpu.VMEM)


def pack_side(projected, mask, narrow, first, count, put):
    sequences, cols = mask.shape
    members = LANES // narrow
    lane = iota((sequences, LANES), 1)
    groups = count // members
    width = groups * LANES
    residue = first + iota((cols, width), 1) // narrow
    masks = matmul(mask, (iota((cols, width), 0) == residue).astype(BF16))
    for group in range(groups):
        value = None
        for member in range(members):
            part = projected[pl.ds(first + group * members + member, sequences, stride=cols), :]
            value = part if value is None else jnp.where(lane >= member * narrow, part, value)
        put(group, (value * masks[:, group * LANES : (group + 1) * LANES]).astype(BF16))
    at = iota((cols, LANES), 1)
    pick = (iota((cols, LANES), 0) - first == at) & (at < count)
    put(groups, matmul(mask, pick.astype(BF16)).astype(BF16))


def side_kernel(
    narrow, align_hbm, mask_hbm, left_w_hbm, right_w_hbm, right_hbm, left_ref,
    left_rows, right_rows, align, mask_int, left_w, right_w, packed, align_sem, mask_sem, left_sem, right_sem, out_sem,
):
    fetches = [
        pltpu.make_async_copy(left_w_hbm, left_w, left_sem),
        pltpu.make_async_copy(right_w_hbm, right_w, right_sem),
        pltpu.make_async_copy(align_hbm, align, align_sem),
        pltpu.make_async_copy(mask_hbm, mask_int, mask_sem),
    ]
    for copy in fetches:
        copy.start()
    for copy in fetches:
        copy.wait()
    members = LANES // narrow
    both = jnp.concatenate([left_w[...]] * members + [right_w[...]] * members, axis=0)
    normed = normalize(align[...].astype(F32)).astype(BF16)
    value = matmul(normed, both, NT)
    left_rows[...] = value[:, :LANES]
    right_rows[...] = value[:, LANES:]
    mask = mask_int[...].astype(BF16)
    cols = mask.shape[1]
    parts = packed.shape[0]
    for h in range(parts):

        def put_right(group, value):
            packed[h, :, group * LANES : (group + 1) * LANES] = value

        pack_side(right_rows, mask, narrow, h * (cols // parts), cols // parts, put_right)
    copies = [
        pltpu.make_async_copy(packed.at[n % parts], right_hbm.at[n], out_sem.at[n])
        for n in range(right_hbm.shape[0])
    ]
    for copy in copies:
        copy.start()

    def put_left(group, value):
        left_ref[:, group * LANES : (group + 1) * LANES] = value

    pack_side(left_rows, mask, narrow, 0, cols, put_left)
    for copy in copies:
        copy.wait()


def prepare_kernel(own, residue_ref, tri_ref, pair_ref, *refs):
    *given_refs, block_ref, tri_rows_ref, pair_mask_ref = refs
    rows, cols, _ = pair_ref.shape
    parts = cols // rows
    row = lax.axis_index("row")
    x = lax.rem(row, parts)
    present = residue_ref[...].astype(BF16)
    residue = iota((present.shape[1], 1), 0)
    place = iota((1, pair_mask_ref.shape[1]), 1)
    tall = lax.div(row, parts) * cols + place % cols
    short = lax.axis_index("col") * cols + x * rows + place // cols
    pair_mask_ref[...] = matmul(present, (residue == tall).astype(BF16)) * matmul(
        present, (residue == short).astype(BF16)
    )
    for i in range(rows):
        at = pl.ds(pl.multiple_of((x * rows + i) * rows, 8), rows)
        block_ref[at, :] = pair_ref[i, pl.ds(pl.multiple_of(x * rows, 8), rows), :]
        for d, given_ref in enumerate(given_refs, 1):
            at = pl.ds(pl.multiple_of((lax.rem(x - d + parts, parts) * rows + i) * rows, 8), rows)
            block_ref[at, :] = given_ref[i]
    out = tri_ref.shape[0]
    at = iota((4 * out, 4 * out), 0)
    kind, rest = at // (2 * out), at % (2 * out)
    owner, side, channel = rest // (2 * own), rest // own % 2, rest % own
    column = side * 2 * out + kind * out + owner * own + channel
    pick = (iota((4 * out, 4 * out), 1) == column).astype(BF16)
    tri_rows_ref[...] = matmul(pick, tri_ref[...], NT).astype(BF16)


def outer_kernel(tall, short, narrow, parts, right_ref, pair_ref, proj_ref, tri_ref, pair_mask_ref, *refs):
    *left_refs, first_ref, tri_out_ref, left, right_t, proj, stacked, spread, moved, rounded = refs
    sources = len(left_refs) // parts
    sequences = left_refs[0].shape[0]
    x, column = lax.rem(lax.axis_index("row"), parts), lax.axis_index("col")
    for n, left_ref in enumerate(left_refs):
        d, k = n // sources, n % sources
        start = (source(column, k, sources) * parts + lax.rem(x - d + parts, parts)) * sequences
        left[pl.ds(pl.multiple_of(start, sequences), sequences), :] = left_ref[...]
    members = LANES // narrow
    groups = tall // members
    left_width, right_width = tall * narrow, short * narrow
    width = pair_ref.shape[1]
    planes = right_t.shape[0]
    for p in range(planes):
        right_t[p] = right_ref[p * LANES : (p + 1) * LANES, :right_width].astype(F32).T
    proj[...] = proj_ref[...].astype(F32)
    steps = stacked.shape[0]
    step = narrow // steps
    spread[...] = jnp.zeros_like(spread)
    total = None
    for n in range(steps):
        some = []
        for p in range(planes):
            each = [right_t.at[p][pl.ds(n * step + d, short, stride=narrow), :] for d in range(step)]
            some.append(jnp.concatenate(each, axis=0).astype(BF16))
        block = matmul(jnp.concatenate(some, axis=1), left[:, :left_width])
        for e in range(0, step, 2):
            lanes = slice(e // 2 * LANES, (e // 2 + 1) * LANES)
            for g in range(0, groups, 2):
                pairs = []
                for d in (e, e + 1):
                    two = [
                        block[d * short : (d + 1) * short, (g + m) * LANES : (g + m + 1) * LANES] for m in range(2)
                    ]
                    pairs.append(jnp.concatenate(two, axis=0).astype(BF16))
                for side in range(2):
                    half = slice(side * LANES // 2, (side + 1) * LANES // 2)
                    at = side * groups * short + g * short
                    stacked[n, at : at + 2 * short, lanes] = jnp.concatenate([v[:, half] for v in pairs], axis=1)
        for d in range(step):
            part = proj[pl.ds(n * step + d, narrow, stride=narrow), :].astype(BF16)
            for m in range(members // 2):
                start = d * LANES // 2 + m * narrow
                spread[n % 2, start : start + narrow, m * width : (m + 1) * width] = part
        term = matmul(stacked[n], spread[n % 2])
        total = term if total is None else total + term
    counts = matmul(right_ref[:, right_width:], left[:, left_width:], TN)[:short, :]
    scale = 1.0 / jnp.maximum(counts, 1.0)
    for g in range(groups):
        for m in range(members):
            i = g * members + m
            at = slice(i * short, (i + 1) * short)
            side, n = m // (members // 2), m % (members // 2)
            start = (side * groups + g) * short
            part = total[start : start + short, n * width : (n + 1) * width]
            moved[at, :] = part * scale[:, i : i + 1] + pair_ref[at, :].astype(F32)
    for j in range(short):
        first = moved[pl.ds(j, tall, stride=short), :].astype(BF16)
        first_ref[j * tall : (j + 1) * tall, :] = first
        rounded[j * tall : (j + 1) * tall, :] = first.astype(F32)
    devices, pair, _ = tri_out_ref.shape
    half = devices * pair
    projections = matmul(tri_ref[...], normalize(rounded[...].T, 0).astype(BF16))
    gated = jax.nn.sigmoid(projections[:half]) * projections[half:] * pair_mask_ref[...]
    gated = gated.astype(BF16)
    for d in range(devices):
        tri_out_ref[d] = gated[d * pair : (d + 1) * pair, :]


def triangle_kernel(row_count, col_count, rows, cols, own, given_ref, out_ref, opened, summed):
    pair = 2 * own
    planes = opened.shape[0]
    parts = cols // rows
    each = -(-col_count // planes)
    used = each * cols

    def open_column(c, carry):
        for a in range(col_count):
            lanes = slice(a % each * cols, (a % each + 1) * cols)
            for x in range(parts):
                value = given_ref[(a * parts + x) * col_count + c].astype(F32)
                for k in range(rows):
                    start = pl.multiple_of((c * cols + x * rows + k) * pair, pair)
                    opened[a // each, pl.ds(start, pair), lanes] = value[:, k * cols : (k + 1) * cols]
        return carry

    residues = row_count * rows
    lax.fori_loop(0, col_count, open_column, 0)
    for t in range(own):
        left = [opened.at[p][pl.ds(t, residues, stride=pair), :].astype(BF16) for p in range(planes)]
        right = [opened.at[p][pl.ds(own + t, residues, stride=pair), :].astype(BF16) for p in range(planes)]
        for p in range(planes):
            count = min(used, residues - p * used)
            for q in range(planes):
                total = matmul(left[p], right[q], TN)[:count]
                summed.at[q][pl.ds(p * used * pair + t, count, stride=pair), :] = total

    def close_row(r, carry):
        for c in range(col_count):
            lanes = slice(c % each * cols, (c % each + 1) * cols)
            parts = []
            for i in range(rows):
                start = pl.multiple_of((r * rows + i) * pair, pair)
                parts.append(summed[c // each, pl.ds(start, pair), lanes])
            out_ref[r * col_count + c] = jnp.concatenate(parts, axis=1)[:own].astype(BF16)
        return carry

    lax.fori_loop(0, row_count, close_row, 0)


def partner(index, k, count):
    return index ^ k if count & (count - 1) == 0 else (index + k) % count


def source(index, k, count):
    return index ^ k if count & (count - 1) == 0 else lax.rem(index - k + count, count)


def triangle_by_channel(row_count, col_count, rows, cols, gated):
    devices, pair, places = gated.shape
    own = pair // 2
    gated = lax.all_to_all(gated, ("row", "col"), split_axis=0, concat_axis=0, tiled=True)
    residues = row_count * rows
    planes = -(-col_count // (LANES // cols))
    (summed,) = call(
        functools.partial(triangle_kernel, row_count, col_count, rows, cols, own),
        16,
        [((devices, own, places), BF16)],
        [pltpu.VMEM((planes, residues * pair, LANES), F32)] * 2,
    )(gated)
    summed = lax.all_to_all(summed, ("row", "col"), split_axis=0, concat_axis=0, tiled=True)
    return summed


def triangle_by_residue(row_count, col_count, rows, cols, gated):
    _, pair, places = gated.shape
    both = gated.reshape(2, pair // 2, cols, rows).transpose(0, 3, 2, 1)
    right = lax.all_gather(both[1], "row", axis=0, tiled=True)
    right = lax.all_to_all(right, "col", split_axis=0, concat_axis=1, tiled=True)
    left = lax.all_gather(both[0], "col", axis=1, tiled=True)
    summed = jnp.einsum("ikc,jkc->cij", left, right, preferred_element_type=F32)
    return summed.reshape(1, pair // 2, places).astype(BF16)


def gate_kernel(first_ref, gate_w_ref, *refs):
    *given_refs, first_t_ref, gated_ref, home = refs
    rows, cols, _ = first_ref.shape
    parts = cols // rows
    x = lax.rem(lax.axis_index("row"), parts)
    for j in range(rows):
        value = first_ref[j, pl.ds(pl.multiple_of(x * rows, 8), rows), :]
        home[pl.ds(x * rows + j, rows, stride=cols), :] = value.astype(F32)
        for d, given_ref in enumerate(given_refs, 1):
            at = pl.ds(lax.rem(x - d + parts, parts) * rows + j, rows, stride=cols)
            home[at, :] = given_ref[j].astype(F32)
    first_t = home[...].T
    first_t_ref[...] = first_t
    gated_ref[...] = jax.nn.sigmoid(matmul(gate_w_ref[...].T, normalize(first_t, 0).astype(BF16)))


def tail_kernel(first_ref, gated_ref, summed_ref, out_w_ref, in_ref, back_ref, out_ref, summed):
    own = summed_ref.shape[1]
    for d in range(summed_ref.shape[0]):
        summed[d * own : (d + 1) * own, :] = summed_ref[d].astype(F32)
    normed_sum = normalize(summed[...], 0).astype(BF16)
    update = gated_ref[...] * matmul(out_w_ref[...].T, normed_sum)
    second = (first_ref[...] + update).astype(BF16).astype(F32)
    normed_second = normalize(second, 0).astype(BF16)
    hidden = jnp.maximum(matmul(in_ref[...].T, normed_second), 0.0).astype(BF16)
    result = second + matmul(back_ref[...].T, hidden)
    out_ref[...] = result.T.astype(BF16)


def shards(
    row_count, col_count, alignment, alignment_mask, residue_mask, pair_features, outer_product_left, outer_product_right,
    outer_proj, triangle_proj, triangle_gate, triangle_out, transition_in, transition_out,
):
    rows, cols, width = pair_features.shape
    sequences, _, channels = alignment.shape
    narrow = outer_product_left.shape[1]
    inner = triangle_out.shape[0]
    devices = row_count * col_count
    turns = cols // rows
    places = rows * cols
    r = lax.axis_index("row")
    by_channel = inner % devices == 0
    owners = devices if by_channel else 1
    own = inner // owners
    members = LANES // narrow
    right_lanes = rows * narrow + LANES
    left_lanes = cols * narrow + LANES
    lines = sequences * cols
    pieces = 8 if narrow % 16 == 0 else 1
    x = r % turns

    hbm = pl.BlockSpec(memory_space=pltpu.HBM)
    right, left = call(
        functools.partial(side_kernel, narrow),
        16,
        [((row_count, sequences, right_lanes), BF16), ((sequences, left_lanes), BF16)],
        [
            pltpu.VMEM((lines, LANES), F32),
            pltpu.VMEM((lines, LANES), F32),
            pltpu.VMEM((lines, channels), BF16),
            pltpu.VMEM((sequences, cols), jnp.int32),
            pltpu.VMEM((narrow, channels), BF16),
            pltpu.VMEM((narrow, channels), BF16),
            pltpu.VMEM((turns, sequences, right_lanes), BF16),
            pltpu.SemaphoreType.DMA,
            pltpu.SemaphoreType.DMA,
            pltpu.SemaphoreType.DMA,
            pltpu.SemaphoreType.DMA,
            pltpu.SemaphoreType.DMA((row_count,)),
        ],
        [hbm] * 4,
        (hbm, VMEM),
    )(*in_hbm([alignment.reshape(lines, channels), alignment_mask, outer_product_left.T, outer_product_right.T]))
    right = lax.all_to_all(right, "row", split_axis=0, concat_axis=0, tiled=True)
    right = right.reshape(row_count * sequences, right_lanes)
    places_of = [(row, col) for row in range(row_count) for col in range(col_count)]

    def route(to):
        return [(row * col_count + col, to(row, col)[0] * col_count + to(row, col)[1]) for row, col in places_of]

    def near(d, k):
        return route(lambda row, col: (row // turns * turns + (row + d) % turns, partner(col, k, col_count)))

    def exchange(values):
        given = []
        for d in range(1, turns):
            part = lax.dynamic_slice_in_dim(values, (x + d) % turns * rows, rows, 1)
            given.append(lax.ppermute(part, ("row", "col"), near(d, 0)))
        return given

    turned = route(lambda row, col: (turns * col + row % turns, row // turns))
    left = lax.ppermute(left, ("row", "col"), turned)
    across = [left] + [lax.ppermute(left, ("row", "col"), near(d, 0)) for d in range(1, turns)]
    blocks = {(d, 0): value for d, value in enumerate(across)}
    if col_count & (col_count - 1) == 0:
        bit = col_count // 2
        while bit:
            for d, k in list(blocks):
                blocks[d, k | bit] = lax.ppermute(blocks[d, k], ("row", "col"), near(0, bit))
            bit //= 2
    else:
        for d in range(turns):
            for k in range(1, col_count):
                blocks[d, k] = lax.ppermute(across[d], ("row", "col"), near(0, k))
    lefts = [blocks[d, k] for d in range(turns) for k in range(col_count)]
    pairs = exchange(pair_features)

    block, tri_rows, pair_mask = call(
        functools.partial(prepare_kernel, own),
        16,
        [((places, width), BF16), ((4 * inner, width), BF16), ((1, places), F32)],
        [],
    )(residue_mask.reshape(1, -1), triangle_proj, pair_features, *pairs)

    first, gated = call(
        functools.partial(outer_kernel, cols, rows, narrow, turns),
        24,
        [((places, width), BF16), ((owners, 2 * own, places), BF16)],
        [
            pltpu.VMEM((row_count * sequences, left_lanes), BF16),
            pltpu.VMEM((row_count * sequences // LANES, rows * narrow, LANES), F32),
            pltpu.VMEM((narrow * narrow, width), F32),
            pltpu.VMEM((pieces, cols // members * rows * 2, narrow // pieces * LANES // 2), BF16),
            pltpu.VMEM((2, narrow // pieces * LANES // 2, members // 2 * width), BF16),
            pltpu.VMEM((places, width), F32),
            pltpu.VMEM((places, width), F32),
        ],
    )(right, block, outer_proj, tri_rows, pair_mask, *lefts)

    first = first.reshape(rows, cols, width)
    firsts = exchange(first)
    first_t, gate = call(gate_kernel, 16, [((width, places), F32)] * 2, [pltpu.VMEM((places, width), F32)])(
        first, triangle_gate, *firsts
    )
    triangle = triangle_by_channel if by_channel else triangle_by_residue
    summed = triangle(row_count, col_count, rows, cols, gated)
    (out,) = call(tail_kernel, 16, [((places, width), BF16)], [pltpu.VMEM((inner, places), F32)])(
        first_t, gate, summed, triangle_out, transition_in, transition_out
    )
    return out.reshape(rows, cols, width)


def solution(mesh):
    placed = (
        P("row", "col", None),
        P("row", "col"),
        P(),
        P("row", "col", None),
    ) + (P(),) * 8

    def body(*args):
        return shards(mesh.shape["row"], mesh.shape["col"], *args)

    return jax.shard_map(body, mesh=mesh, in_specs=placed, out_specs=P("row", "col", None), check_vma=False)
```

```python
import functools

import jax
import jax.numpy as jnp
from jax import lax
from jax.experimental import pallas as pl
from jax.experimental.pallas import tpu as pltpu
from jax.sharding import PartitionSpec as P


epsilon = 1e-05
LANES = 128
ABSENT = 2.0**100
BF16 = jnp.bfloat16
F32 = jnp.float32
NT = (((1,), (1,)), ((), ()))
TN = (((0,), (0,)), ((), ()))


def matmul(a, b, dims=(((1,), (0,)), ((), ()))):
    return lax.dot_general(a, b, dims, preferred_element_type=F32)


def iota(shape, axis):
    return lax.broadcasted_iota(jnp.int32, shape, axis)


def normalize(values, axis=-1):
    mean_value = jnp.mean(values, axis=axis, keepdims=True)
    centered = values - mean_value
    variance = jnp.mean(centered * centered, axis=axis, keepdims=True)
    return centered * lax.rsqrt(variance + epsilon)


def in_hbm(values):
    return [pltpu.with_memory_space_constraint(value, pltpu.HBM) for value in values]


def call(kernel, mebibytes, outs, scratch, in_specs=None, out_specs=None):
    return pl.pallas_call(
        kernel,
        out_shape=tuple(jax.ShapeDtypeStruct(*out) for out in outs),
        out_specs=out_specs or (VMEM,) * len(outs),
        scratch_shapes=scratch,
        compiler_params=pltpu.CompilerParams(vmem_limit_bytes=mebibytes * 1024 * 1024),
        **({} if in_specs is None else {"in_specs": in_specs}),
    )


VMEM = pl.BlockSpec(memory_space=pltpu.VMEM)


def pack_side(projected, mask, narrow, first, count, put, marked=False):
    sequences, cols = mask.shape
    members = LANES // narrow
    lane = iota((sequences, LANES), 1)
    groups = count // members
    width = groups * LANES
    residue = first + iota((cols, width), 1) // narrow
    masks = matmul(mask, (iota((cols, width), 0) == residue).astype(BF16))
    for group in range(groups):
        value = None
        for member in range(members):
            part = projected[pl.ds(first + group * members + member, sequences, stride=cols), :]
            value = part if value is None else jnp.where(lane >= member * narrow, part, value)
        kept = masks[:, group * LANES : (group + 1) * LANES]
        put(group, (jnp.where(kept > 0.5, value, ABSENT) if marked else value * kept).astype(BF16))
    if marked:
        return
    at = iota((cols, LANES), 1)
    pick = (iota((cols, LANES), 0) - first == at) & (at < count)
    put(groups, matmul(mask, pick.astype(BF16)).astype(BF16))


def side_kernel(
    narrow, align_hbm, mask_hbm, left_w_hbm, right_w_hbm, right_hbm, left_ref,
    left_rows, right_rows, align, mask_int, left_w, right_w, packed, align_sem, mask_sem, left_sem, right_sem, out_sem,
):
    fetches = [
        pltpu.make_async_copy(left_w_hbm, left_w, left_sem),
        pltpu.make_async_copy(right_w_hbm, right_w, right_sem),
        pltpu.make_async_copy(align_hbm, align, align_sem),
        pltpu.make_async_copy(mask_hbm, mask_int, mask_sem),
    ]
    for copy in fetches:
        copy.start()
    for copy in fetches:
        copy.wait()
    members = LANES // narrow
    both = jnp.concatenate([left_w[...]] * members + [right_w[...]] * members, axis=0)
    normed = normalize(align[...].astype(F32)).astype(BF16)
    value = matmul(normed, both, NT)
    left_rows[...] = value[:, :LANES]
    right_rows[...] = value[:, LANES:]
    mask = mask_int[...].astype(BF16)
    cols = mask.shape[1]
    parts = packed.shape[0]
    for h in range(parts):

        def put_right(group, value):
            packed[h, :, group * LANES : (group + 1) * LANES] = value

        pack_side(right_rows, mask, narrow, h * (cols // parts), cols // parts, put_right, True)
    copies = [
        pltpu.make_async_copy(packed.at[n % parts], right_hbm.at[n], out_sem.at[n])
        for n in range(right_hbm.shape[0])
    ]
    for copy in copies:
        copy.start()

    def put_left(group, value):
        left_ref[:, group * LANES : (group + 1) * LANES] = value

    pack_side(left_rows, mask, narrow, 0, cols, put_left)
    for copy in copies:
        copy.wait()


def prepare_kernel(own, residue_ref, tri_ref, pair_ref, *refs):
    *given_refs, block_ref, tri_rows_ref, pair_mask_ref = refs
    rows, cols, _ = pair_ref.shape
    parts = cols // rows
    row = lax.axis_index("row")
    x = lax.rem(row, parts)
    present = residue_ref[...].astype(BF16)
    residue = iota((present.shape[1], 1), 0)
    place = iota((1, pair_mask_ref.shape[1]), 1)
    tall = lax.div(row, parts) * cols + place % cols
    short = lax.axis_index("col") * cols + x * rows + place // cols
    pair_mask_ref[...] = matmul(present, (residue == tall).astype(BF16)) * matmul(
        present, (residue == short).astype(BF16)
    )
    for i in range(rows):
        at = pl.ds(pl.multiple_of((x * rows + i) * rows, 8), rows)
        block_ref[at, :] = pair_ref[i, pl.ds(pl.multiple_of(x * rows, 8), rows), :]
        for d, given_ref in enumerate(given_refs, 1):
            at = pl.ds(pl.multiple_of((lax.rem(x - d + parts, parts) * rows + i) * rows, 8), rows)
            block_ref[at, :] = given_ref[i]
    out = tri_ref.shape[0]
    at = iota((4 * out, 4 * out), 0)
    kind, rest = at // (2 * out), at % (2 * out)
    owner, side, channel = rest // (2 * own), rest // own % 2, rest % own
    column = side * 2 * out + kind * out + owner * own + channel
    pick = (iota((4 * out, 4 * out), 1) == column).astype(BF16)
    tri_rows_ref[...] = matmul(pick, tri_ref[...], NT).astype(BF16)


def outer_kernel(tall, short, narrow, parts, right_ref, pair_ref, proj_ref, tri_ref, pair_mask_ref, *refs):
    *left_refs, first_ref, tri_out_ref, left, right_t, proj, stacked, spread, moved, rounded = refs
    sources = len(left_refs) // parts
    sequences = left_refs[0].shape[0]
    x, column = lax.rem(lax.axis_index("row"), parts), lax.axis_index("col")
    for n, left_ref in enumerate(left_refs):
        d, k = n // sources, n % sources
        start = (source(column, k, sources) * parts + lax.rem(x - d + parts, parts)) * sequences
        left[pl.ds(pl.multiple_of(start, sequences), sequences), :] = left_ref[...]
    members = LANES // narrow
    groups = tall // members
    left_width = tall * narrow
    width = pair_ref.shape[1]
    planes = right_t.shape[0]
    for p in range(planes):
        right_t[p] = right_ref[p * LANES : (p + 1) * LANES, :].astype(F32).T
    proj[...] = proj_ref[...].astype(F32)
    steps = stacked.shape[0]
    step = narrow // steps
    spread[...] = jnp.zeros_like(spread)
    total = None
    for n in range(steps):
        some = []
        for p in range(planes):
            each = [right_t.at[p][pl.ds(n * step + d, short, stride=narrow), :] for d in range(step)]
            each = jnp.concatenate(each, axis=0)
            some.append(jnp.where(each < ABSENT / 2, each, 0.0).astype(BF16))
        block = matmul(jnp.concatenate(some, axis=1), left[:, :left_width])
        for e in range(0, step, 2):
            lanes = slice(e // 2 * LANES, (e // 2 + 1) * LANES)
            for g in range(0, groups, 2):
                pairs = []
                for d in (e, e + 1):
                    two = [
                        block[d * short : (d + 1) * short, (g + m) * LANES : (g + m + 1) * LANES] for m in range(2)
                    ]
                    pairs.append(jnp.concatenate(two, axis=0).astype(BF16))
                for side in range(2):
                    half = slice(side * LANES // 2, (side + 1) * LANES // 2)
                    at = side * groups * short + g * short
                    stacked[n, at : at + 2 * short, lanes] = jnp.concatenate([v[:, half] for v in pairs], axis=1)
        for d in range(step):
            part = proj[pl.ds(n * step + d, narrow, stride=narrow), :].astype(BF16)
            for m in range(members // 2):
                start = d * LANES // 2 + m * narrow
                spread[n % 2, start : start + narrow, m * width : (m + 1) * width] = part
        term = matmul(stacked[n], spread[n % 2])
        total = term if total is None else total + term
    present = [right_t.at[p][pl.ds(0, short, stride=narrow), :] < ABSENT / 2 for p in range(planes)]
    counts = matmul(jnp.concatenate(present, axis=1).astype(BF16), left[:, left_width:])
    scale = 1.0 / jnp.maximum(counts, 1.0)
    for g in range(groups):
        for m in range(members):
            i = g * members + m
            at = slice(i * short, (i + 1) * short)
            side, n = m // (members // 2), m % (members // 2)
            start = (side * groups + g) * short
            part = total[start : start + short, n * width : (n + 1) * width]
            moved[at, :] = part * scale[:, i : i + 1] + pair_ref[at, :].astype(F32)
    for j in range(short):
        first = moved[pl.ds(j, tall, stride=short), :].astype(BF16)
        first_ref[j * tall : (j + 1) * tall, :] = first
        rounded[j * tall : (j + 1) * tall, :] = first.astype(F32)
    devices, pair, _ = tri_out_ref.shape
    half = devices * pair
    projections = matmul(tri_ref[...], normalize(rounded[...].T, 0).astype(BF16))
    gated = jax.nn.sigmoid(projections[:half]) * projections[half:] * pair_mask_ref[...]
    gated = gated.astype(BF16)
    for d in range(devices):
        tri_out_ref[d] = gated[d * pair : (d + 1) * pair, :]


def triangle_kernel(row_count, col_count, rows, cols, own, given_ref, out_ref, opened, summed):
    pair = 2 * own
    planes = opened.shape[0]
    parts = cols // rows
    each = -(-col_count // planes)
    used = each * cols

    def open_column(c, carry):
        for a in range(col_count):
            lanes = slice(a % each * cols, (a % each + 1) * cols)
            for x in range(parts):
                value = given_ref[(a * parts + x) * col_count + c].astype(F32)
                for k in range(rows):
                    start = pl.multiple_of((c * cols + x * rows + k) * pair, pair)
                    opened[a // each, pl.ds(start, pair), lanes] = value[:, k * cols : (k + 1) * cols]
        return carry

    residues = row_count * rows
    folds = 2 if planes == 2 and residues == 2 * used else 1
    lax.fori_loop(0, col_count, open_column, 0)
    for t in range(own):
        left = [opened.at[p][pl.ds(t, residues, stride=pair), :].astype(BF16) for p in range(planes)]
        right = [opened.at[p][pl.ds(own + t, residues, stride=pair), :].astype(BF16) for p in range(planes)]
        for p in range(planes):
            count = min(used, residues - p * used)
            for q in range(planes):
                total = matmul(left[p], right[q], TN)[:count]
                start = p * own if folds == 2 else p * used * pair
                summed.at[q][pl.ds(start + t, count, stride=pair), :] = total

    def close_row(r, carry):
        for c in range(col_count):
            lanes = slice(c % each * cols, (c % each + 1) * cols)
            parts = []
            for i in range(rows):
                start = pl.multiple_of((r * rows + i) * pair, pair)
                parts.append(summed[c // each, pl.ds(start, pair), lanes])
            value = jnp.concatenate(parts, axis=1)
            for fold in range(folds):
                at = (r + fold * (row_count // folds)) * col_count + c
                out_ref[at] = value[fold * own : (fold + 1) * own].astype(BF16)
        return carry

    lax.fori_loop(0, row_count // folds, close_row, 0)


def partner(index, k, count):
    return index ^ k if count & (count - 1) == 0 else (index + k) % count


def source(index, k, count):
    return index ^ k if count & (count - 1) == 0 else lax.rem(index - k + count, count)


def triangle_by_channel(row_count, col_count, rows, cols, gated):
    devices, pair, places = gated.shape
    own = pair // 2
    gated = lax.all_to_all(gated, ("row", "col"), split_axis=0, concat_axis=0, tiled=True)
    residues = row_count * rows
    planes = -(-col_count // (LANES // cols))
    (summed,) = call(
        functools.partial(triangle_kernel, row_count, col_count, rows, cols, own),
        16,
        [((devices, own, places), BF16)],
        [pltpu.VMEM((planes, residues * pair, LANES), F32)] * 2,
    )(gated)
    summed = lax.all_to_all(summed, ("row", "col"), split_axis=0, concat_axis=0, tiled=True)
    return summed


def triangle_by_residue(row_count, col_count, rows, cols, gated):
    _, pair, places = gated.shape
    both = gated.reshape(2, pair // 2, cols, rows).transpose(0, 3, 2, 1)
    right = lax.all_gather(both[1], "row", axis=0, tiled=True)
    right = lax.all_to_all(right, "col", split_axis=0, concat_axis=1, tiled=True)
    left = lax.all_gather(both[0], "col", axis=1, tiled=True)
    summed = jnp.einsum("ikc,jkc->cij", left, right, preferred_element_type=F32)
    return summed.reshape(1, pair // 2, places).astype(BF16)


def gate_kernel(first_ref, gate_w_ref, *refs):
    *given_refs, first_t_ref, gated_ref, home = refs
    rows, cols, _ = first_ref.shape
    parts = cols // rows
    x = lax.rem(lax.axis_index("row"), parts)
    for j in range(rows):
        value = first_ref[j, pl.ds(pl.multiple_of(x * rows, 8), rows), :]
        home[pl.ds(x * rows + j, rows, stride=cols), :] = value.astype(F32)
        for d, given_ref in enumerate(given_refs, 1):
            at = pl.ds(lax.rem(x - d + parts, parts) * rows + j, rows, stride=cols)
            home[at, :] = given_ref[j].astype(F32)
    first_t = home[...].T
    first_t_ref[...] = first_t
    gated_ref[...] = jax.nn.sigmoid(matmul(gate_w_ref[...].T, normalize(first_t, 0).astype(BF16)))


def tail_kernel(first_ref, gated_ref, summed_ref, out_w_ref, in_ref, back_ref, out_ref, summed):
    own = summed_ref.shape[1]
    for d in range(summed_ref.shape[0]):
        summed[d * own : (d + 1) * own, :] = summed_ref[d].astype(F32)
    normed_sum = normalize(summed[...], 0).astype(BF16)
    update = gated_ref[...] * matmul(out_w_ref[...].T, normed_sum)
    second = (first_ref[...] + update).astype(BF16).astype(F32)
    normed_second = normalize(second, 0).astype(BF16)
    hidden = jnp.maximum(matmul(in_ref[...].T, normed_second), 0.0).astype(BF16)
    result = second + matmul(back_ref[...].T, hidden)
    out_ref[...] = result.T.astype(BF16)


def shards(
    row_count, col_count, alignment, alignment_mask, residue_mask, pair_features, outer_product_left, outer_product_right,
    outer_proj, triangle_proj, triangle_gate, triangle_out, transition_in, transition_out,
):
    rows, cols, width = pair_features.shape
    sequences, _, channels = alignment.shape
    narrow = outer_product_left.shape[1]
    inner = triangle_out.shape[0]
    devices = row_count * col_count
    turns = cols // rows
    places = rows * cols
    r = lax.axis_index("row")
    by_channel = inner % devices == 0
    owners = devices if by_channel else 1
    own = inner // owners
    members = LANES // narrow
    right_lanes = rows * narrow
    left_lanes = cols * narrow + LANES
    lines = sequences * cols
    pieces = 8 if narrow % 16 == 0 else 1
    x = r % turns

    hbm = pl.BlockSpec(memory_space=pltpu.HBM)
    right, left = call(
        functools.partial(side_kernel, narrow),
        16,
        [((row_count, sequences, right_lanes), BF16), ((sequences, left_lanes), BF16)],
        [
            pltpu.VMEM((lines, LANES), F32),
            pltpu.VMEM((lines, LANES), F32),
            pltpu.VMEM((lines, channels), BF16),
            pltpu.VMEM((sequences, cols), jnp.int32),
            pltpu.VMEM((narrow, channels), BF16),
            pltpu.VMEM((narrow, channels), BF16),
            pltpu.VMEM((turns, sequences, right_lanes), BF16),
            pltpu.SemaphoreType.DMA,
            pltpu.SemaphoreType.DMA,
            pltpu.SemaphoreType.DMA,
            pltpu.SemaphoreType.DMA,
            pltpu.SemaphoreType.DMA((row_count,)),
        ],
        [hbm] * 4,
        (hbm, VMEM),
    )(*in_hbm([alignment.reshape(lines, channels), alignment_mask, outer_product_left.T, outer_product_right.T]))
    right = lax.all_to_all(right, "row", split_axis=0, concat_axis=0, tiled=True)
    right = right.reshape(row_count * sequences, right_lanes)
    places_of = [(row, col) for row in range(row_count) for col in range(col_count)]

    def route(to):
        return [(row * col_count + col, to(row, col)[0] * col_count + to(row, col)[1]) for row, col in places_of]

    def near(d, k):
        return route(lambda row, col: (row // turns * turns + (row + d) % turns, partner(col, k, col_count)))

    def exchange(values):
        given = []
        for d in range(1, turns):
            part = lax.dynamic_slice_in_dim(values, (x + d) % turns * rows, rows, 1)
            given.append(lax.ppermute(part, ("row", "col"), near(d, 0)))
        return given

    turned = route(lambda row, col: (turns * col + row % turns, row // turns))
    left = lax.ppermute(left, ("row", "col"), turned)
    across = [left] + [lax.ppermute(left, ("row", "col"), near(d, 0)) for d in range(1, turns)]
    blocks = {(d, 0): value for d, value in enumerate(across)}
    if col_count & (col_count - 1) == 0:
        bit = col_count // 2
        while bit:
            for d, k in list(blocks):
                blocks[d, k | bit] = lax.ppermute(blocks[d, k], ("row", "col"), near(0, bit))
            bit //= 2
    else:
        for d in range(turns):
            for k in range(1, col_count):
                blocks[d, k] = lax.ppermute(across[d], ("row", "col"), near(0, k))
    lefts = [blocks[d, k] for d in range(turns) for k in range(col_count)]
    pairs = exchange(pair_features)

    block, tri_rows, pair_mask = call(
        functools.partial(prepare_kernel, own),
        16,
        [((places, width), BF16), ((4 * inner, width), BF16), ((1, places), F32)],
        [],
    )(residue_mask.reshape(1, -1), triangle_proj, pair_features, *pairs)

    first, gated = call(
        functools.partial(outer_kernel, cols, rows, narrow, turns),
        24,
        [((places, width), BF16), ((owners, 2 * own, places), BF16)],
        [
            pltpu.VMEM((row_count * sequences, left_lanes), BF16),
            pltpu.VMEM((row_count * sequences // LANES, rows * narrow, LANES), F32),
            pltpu.VMEM((narrow * narrow, width), F32),
            pltpu.VMEM((pieces, cols // members * rows * 2, narrow // pieces * LANES // 2), BF16),
            pltpu.VMEM((2, narrow // pieces * LANES // 2, members // 2 * width), BF16),
            pltpu.VMEM((places, width), F32),
            pltpu.VMEM((places, width), F32),
        ],
    )(right, block, outer_proj, tri_rows, pair_mask, *lefts)

    first = first.reshape(rows, cols, width)
    firsts = exchange(first)
    first_t, gate = call(gate_kernel, 16, [((width, places), F32)] * 2, [pltpu.VMEM((places, width), F32)])(
        first, triangle_gate, *firsts
    )
    triangle = triangle_by_channel if by_channel else triangle_by_residue
    summed = triangle(row_count, col_count, rows, cols, gated)
    (out,) = call(tail_kernel, 16, [((places, width), BF16)], [pltpu.VMEM((inner, places), F32)])(
        first_t, gate, summed, triangle_out, transition_in, transition_out
    )
    return out.reshape(rows, cols, width)


def solution(mesh):
    placed = (
        P("row", "col", None),
        P("row", "col"),
        P(),
        P("row", "col", None),
    ) + (P(),) * 8

    def body(*args):
        return shards(mesh.shape["row"], mesh.shape["col"], *args)

    return jax.shard_map(body, mesh=mesh, in_specs=placed, out_specs=P("row", "col", None), check_vma=False)
```

```python
import functools

import jax
import jax.numpy as jnp
from jax import lax
from jax.experimental import pallas as pl
from jax.experimental.pallas import tpu as pltpu
from jax.sharding import PartitionSpec as P


epsilon = 1e-05
LANES = 128
ABSENT = 2.0**100
BF16 = jnp.bfloat16
F32 = jnp.float32
NT = (((1,), (1,)), ((), ()))
TN = (((0,), (0,)), ((), ()))


def matmul(a, b, dims=(((1,), (0,)), ((), ()))):
    return lax.dot_general(a, b, dims, preferred_element_type=F32)


def iota(shape, axis):
    return lax.broadcasted_iota(jnp.int32, shape, axis)


def normalize(values, axis=-1):
    mean_value = jnp.mean(values, axis=axis, keepdims=True)
    centered = values - mean_value
    variance = jnp.mean(centered * centered, axis=axis, keepdims=True)
    return centered * lax.rsqrt(variance + epsilon)


def in_hbm(values):
    return [pltpu.with_memory_space_constraint(value, pltpu.HBM) for value in values]


def call(kernel, mebibytes, outs, scratch, in_specs=None, out_specs=None):
    return pl.pallas_call(
        kernel,
        out_shape=tuple(jax.ShapeDtypeStruct(*out) for out in outs),
        out_specs=out_specs or (VMEM,) * len(outs),
        scratch_shapes=scratch,
        compiler_params=pltpu.CompilerParams(vmem_limit_bytes=mebibytes * 1024 * 1024),
        **({} if in_specs is None else {"in_specs": in_specs}),
    )


VMEM = pl.BlockSpec(memory_space=pltpu.VMEM)


def pack_side(projected, mask, narrow, first, count, put, marked=False):
    sequences, cols = mask.shape
    members = LANES // narrow
    lane = iota((sequences, LANES), 1)
    groups = count // members
    width = groups * LANES
    residue = first + iota((cols, width), 1) // narrow
    masks = matmul(mask, (iota((cols, width), 0) == residue).astype(BF16))
    for group in range(groups):
        value = None
        for member in range(members):
            part = projected[pl.ds(first + group * members + member, sequences, stride=cols), :]
            value = part if value is None else jnp.where(lane >= member * narrow, part, value)
        kept = masks[:, group * LANES : (group + 1) * LANES]
        put(group, (jnp.where(kept > 0.5, value, ABSENT) if marked else value * kept).astype(BF16))
    if marked:
        return
    at = iota((cols, LANES), 1)
    pick = (iota((cols, LANES), 0) - first == at) & (at < count)
    put(groups, matmul(mask, pick.astype(BF16)).astype(BF16))


def side_kernel(
    narrow, align_hbm, mask_hbm, left_w_hbm, right_w_hbm, right_hbm, left_ref,
    left_rows, right_rows, align, mask_int, left_w, right_w, packed, align_sem, mask_sem, left_sem, right_sem, out_sem,
):
    fetches = [
        pltpu.make_async_copy(left_w_hbm, left_w, left_sem),
        pltpu.make_async_copy(right_w_hbm, right_w, right_sem),
        pltpu.make_async_copy(align_hbm, align, align_sem),
        pltpu.make_async_copy(mask_hbm, mask_int, mask_sem),
    ]
    for copy in fetches:
        copy.start()
    for copy in fetches:
        copy.wait()
    members = LANES // narrow
    both = jnp.concatenate([left_w[...]] * members + [right_w[...]] * members, axis=0)
    normed = normalize(align[...].astype(F32)).astype(BF16)
    value = matmul(normed, both, NT)
    left_rows[...] = value[:, :LANES]
    right_rows[...] = value[:, LANES:]
    mask = mask_int[...].astype(BF16)
    cols = mask.shape[1]
    parts = packed.shape[0]
    for h in range(parts):

        def put_right(group, value):
            packed[h, :, group * LANES : (group + 1) * LANES] = value

        pack_side(right_rows, mask, narrow, h * (cols // parts), cols // parts, put_right, True)
    copies = [
        pltpu.make_async_copy(packed.at[n % parts], right_hbm.at[n], out_sem.at[n])
        for n in range(right_hbm.shape[0])
    ]
    for copy in copies:
        copy.start()

    def put_left(group, value):
        left_ref[:, group * LANES : (group + 1) * LANES] = value

    pack_side(left_rows, mask, narrow, 0, cols, put_left)
    for copy in copies:
        copy.wait()


def prepare_kernel(own, residue_ref, tri_ref, pair_ref, *refs):
    *given_refs, block_ref, tri_rows_ref, pair_mask_ref = refs
    rows, cols, _ = pair_ref.shape
    parts = cols // rows
    row = lax.axis_index("row")
    x = lax.rem(row, parts)
    present = residue_ref[...].astype(BF16)
    residue = iota((present.shape[1], 1), 0)
    place = iota((1, pair_mask_ref.shape[1]), 1)
    tall = lax.div(row, parts) * cols + place % cols
    short = lax.axis_index("col") * cols + x * rows + place // cols
    pair_mask_ref[...] = matmul(present, (residue == tall).astype(BF16)) * matmul(
        present, (residue == short).astype(BF16)
    )
    for i in range(rows):
        at = pl.ds(pl.multiple_of((x * rows + i) * rows, 8), rows)
        block_ref[at, :] = pair_ref[i, pl.ds(pl.multiple_of(x * rows, 8), rows), :]
        for d, given_ref in enumerate(given_refs, 1):
            at = pl.ds(pl.multiple_of((lax.rem(x - d + parts, parts) * rows + i) * rows, 8), rows)
            block_ref[at, :] = given_ref[i]
    out = tri_ref.shape[0]
    at = iota((4 * out, 4 * out), 0)
    kind, rest = at // (2 * out), at % (2 * out)
    owner, side, channel = rest // (2 * own), rest // own % 2, rest % own
    column = side * 2 * out + kind * out + owner * own + channel
    pick = (iota((4 * out, 4 * out), 1) == column).astype(BF16)
    tri_rows_ref[...] = matmul(pick, tri_ref[...], NT).astype(BF16)


def outer_kernel(tall, short, narrow, parts, right_ref, pair_ref, proj_ref, tri_ref, pair_mask_ref, *refs):
    *left_refs, first_ref, tri_out_ref, left, right_t, proj, stacked, spread, moved, rounded = refs
    sources = len(left_refs) // parts
    sequences = left_refs[0].shape[0]
    x, column = lax.rem(lax.axis_index("row"), parts), lax.axis_index("col")
    for n, left_ref in enumerate(left_refs):
        d, k = n // sources, n % sources
        plane = turned_column(source(column, k, sources), sources)
        start = (plane * parts + lax.rem(x - d + parts, parts)) * sequences
        left[pl.ds(pl.multiple_of(start, sequences), sequences), :] = left_ref[...]
    members = LANES // narrow
    groups = tall // members
    left_width = tall * narrow
    width = pair_ref.shape[1]
    planes = right_t.shape[0]
    for p in range(planes):
        right_t[p] = right_ref[p * LANES : (p + 1) * LANES, :].astype(F32).T
    proj[...] = proj_ref[...].astype(F32)
    steps = stacked.shape[0]
    step = narrow // steps
    spread[...] = jnp.zeros_like(spread)
    total = None
    for n in range(steps):
        some = []
        for p in range(planes):
            each = [right_t.at[p][pl.ds(n * step + d, short, stride=narrow), :] for d in range(step)]
            each = jnp.concatenate(each, axis=0)
            some.append(jnp.where(each < ABSENT / 2, each, 0.0).astype(BF16))
        block = matmul(jnp.concatenate(some, axis=1), left[:, :left_width])
        for e in range(0, step, 2):
            lanes = slice(e // 2 * LANES, (e // 2 + 1) * LANES)
            for g in range(0, groups, 2):
                pairs = []
                for d in (e, e + 1):
                    two = [
                        block[d * short : (d + 1) * short, (g + m) * LANES : (g + m + 1) * LANES] for m in range(2)
                    ]
                    pairs.append(jnp.concatenate(two, axis=0).astype(BF16))
                for side in range(2):
                    half = slice(side * LANES // 2, (side + 1) * LANES // 2)
                    at = side * groups * short + g * short
                    stacked[n, at : at + 2 * short, lanes] = jnp.concatenate([v[:, half] for v in pairs], axis=1)
        for d in range(step):
            part = proj[pl.ds(n * step + d, narrow, stride=narrow), :].astype(BF16)
            for m in range(members // 2):
                start = d * LANES // 2 + m * narrow
                spread[n % 2, start : start + narrow, m * width : (m + 1) * width] = part
        term = matmul(stacked[n], spread[n % 2])
        total = term if total is None else total + term
    present = [right_t.at[p][pl.ds(0, short, stride=narrow), :] < ABSENT / 2 for p in range(planes)]
    counts = matmul(jnp.concatenate(present, axis=1).astype(BF16), left[:, left_width:])
    scale = 1.0 / jnp.maximum(counts, 1.0)
    for g in range(groups):
        for m in range(members):
            i = g * members + m
            at = slice(i * short, (i + 1) * short)
            side, n = m // (members // 2), m % (members // 2)
            start = (side * groups + g) * short
            part = total[start : start + short, n * width : (n + 1) * width]
            moved[at, :] = part * scale[:, i : i + 1] + pair_ref[at, :].astype(F32)
    for j in range(short):
        first = moved[pl.ds(j, tall, stride=short), :].astype(BF16)
        first_ref[j * tall : (j + 1) * tall, :] = first
        rounded[j * tall : (j + 1) * tall, :] = first.astype(F32)
    devices, pair, _ = tri_out_ref.shape
    half = devices * pair
    projections = matmul(tri_ref[...], normalize(rounded[...].T, 0).astype(BF16))
    gated = jax.nn.sigmoid(projections[:half]) * projections[half:] * pair_mask_ref[...]
    gated = gated.astype(BF16)
    for d in range(devices):
        tri_out_ref[d] = gated[d * pair : (d + 1) * pair, :]


def triangle_kernel(row_count, col_count, rows, cols, own, given_ref, out_ref, opened, summed):
    pair = 2 * own
    planes = opened.shape[0]
    parts = cols // rows
    each = -(-col_count // planes)
    used = each * cols

    def open_column(c, carry):
        for a in range(col_count):
            lanes = slice(a % each * cols, (a % each + 1) * cols)
            for x in range(parts):
                value = given_ref[(a * parts + x) * col_count + c].astype(F32)
                for k in range(rows):
                    start = pl.multiple_of((c * cols + x * rows + k) * pair, pair)
                    opened[a // each, pl.ds(start, pair), lanes] = value[:, k * cols : (k + 1) * cols]
        return carry

    residues = row_count * rows
    folds = 2 if planes == 2 and residues == 2 * used else 1
    lax.fori_loop(0, col_count, open_column, 0)
    for t in range(own):
        left = [opened.at[p][pl.ds(t, residues, stride=pair), :].astype(BF16) for p in range(planes)]
        right = [opened.at[p][pl.ds(own + t, residues, stride=pair), :].astype(BF16) for p in range(planes)]
        for p in range(planes):
            count = min(used, residues - p * used)
            for q in range(planes):
                total = matmul(left[p], right[q], TN)[:count]
                start = p * own if folds == 2 else p * used * pair
                summed.at[q][pl.ds(start + t, count, stride=pair), :] = total

    def close_row(r, carry):
        for c in range(col_count):
            lanes = slice(c % each * cols, (c % each + 1) * cols)
            parts = []
            for i in range(rows):
                start = pl.multiple_of((r * rows + i) * pair, pair)
                parts.append(summed[c // each, pl.ds(start, pair), lanes])
            value = jnp.concatenate(parts, axis=1)
            for fold in range(folds):
                at = (r + fold * (row_count // folds)) * col_count + c
                out_ref[at] = value[fold * own : (fold + 1) * own].astype(BF16)
        return carry

    lax.fori_loop(0, row_count // folds, close_row, 0)


def partner(index, k, count):
    return index ^ k if count & (count - 1) == 0 else (index + k) % count


def turned_column(plane, count):
    return plane ^ (count // 2) if count & (count - 1) == 0 else plane


def source(index, k, count):
    return index ^ k if count & (count - 1) == 0 else lax.rem(index - k + count, count)


def triangle_by_channel(row_count, col_count, rows, cols, gated):
    devices, pair, places = gated.shape
    own = pair // 2
    gated = lax.all_to_all(gated, ("row", "col"), split_axis=0, concat_axis=0, tiled=True)
    residues = row_count * rows
    planes = -(-col_count // (LANES // cols))
    (summed,) = call(
        functools.partial(triangle_kernel, row_count, col_count, rows, cols, own),
        16,
        [((devices, own, places), BF16)],
        [pltpu.VMEM((planes, residues * pair, LANES), F32)] * 2,
    )(gated)
    summed = lax.all_to_all(summed, ("row", "col"), split_axis=0, concat_axis=0, tiled=True)
    return summed


def triangle_by_residue(row_count, col_count, rows, cols, gated):
    _, pair, places = gated.shape
    both = gated.reshape(2, pair // 2, cols, rows).transpose(0, 3, 2, 1)
    right = lax.all_gather(both[1], "row", axis=0, tiled=True)
    right = lax.all_to_all(right, "col", split_axis=0, concat_axis=1, tiled=True)
    left = lax.all_gather(both[0], "col", axis=1, tiled=True)
    summed = jnp.einsum("ikc,jkc->cij", left, right, preferred_element_type=F32)
    return summed.reshape(1, pair // 2, places).astype(BF16)


def gate_kernel(first_ref, gate_w_ref, *refs):
    *given_refs, first_t_ref, gated_ref, home = refs
    rows, cols, _ = first_ref.shape
    parts = cols // rows
    x = lax.rem(lax.axis_index("row"), parts)
    for j in range(rows):
        value = first_ref[j, pl.ds(pl.multiple_of(x * rows, 8), rows), :]
        home[pl.ds(x * rows + j, rows, stride=cols), :] = value.astype(F32)
        for d, given_ref in enumerate(given_refs, 1):
            at = pl.ds(lax.rem(x - d + parts, parts) * rows + j, rows, stride=cols)
            home[at, :] = given_ref[j].astype(F32)
    first_t = home[...].T
    first_t_ref[...] = first_t
    gated_ref[...] = jax.nn.sigmoid(matmul(gate_w_ref[...].T, normalize(first_t, 0).astype(BF16)))


def tail_kernel(first_ref, gated_ref, summed_ref, out_w_ref, in_ref, back_ref, out_ref, summed):
    own = summed_ref.shape[1]
    for d in range(summed_ref.shape[0]):
        summed[d * own : (d + 1) * own, :] = summed_ref[d].astype(F32)
    normed_sum = normalize(summed[...], 0).astype(BF16)
    update = gated_ref[...] * matmul(out_w_ref[...].T, normed_sum)
    second = (first_ref[...] + update).astype(BF16).astype(F32)
    normed_second = normalize(second, 0).astype(BF16)
    hidden = jnp.maximum(matmul(in_ref[...].T, normed_second), 0.0).astype(BF16)
    result = second + matmul(back_ref[...].T, hidden)
    out_ref[...] = result.T.astype(BF16)


def shards(
    row_count, col_count, alignment, alignment_mask, residue_mask, pair_features, outer_product_left, outer_product_right,
    outer_proj, triangle_proj, triangle_gate, triangle_out, transition_in, transition_out,
):
    rows, cols, width = pair_features.shape
    sequences, _, channels = alignment.shape
    narrow = outer_product_left.shape[1]
    inner = triangle_out.shape[0]
    devices = row_count * col_count
    turns = cols // rows
    places = rows * cols
    r = lax.axis_index("row")
    by_channel = inner % devices == 0
    owners = devices if by_channel else 1
    own = inner // owners
    members = LANES // narrow
    right_lanes = rows * narrow
    left_lanes = cols * narrow + LANES
    lines = sequences * cols
    pieces = 8 if narrow % 16 == 0 else 1
    x = r % turns

    hbm = pl.BlockSpec(memory_space=pltpu.HBM)
    right, left = call(
        functools.partial(side_kernel, narrow),
        16,
        [((row_count, sequences, right_lanes), BF16), ((sequences, left_lanes), BF16)],
        [
            pltpu.VMEM((lines, LANES), F32),
            pltpu.VMEM((lines, LANES), F32),
            pltpu.VMEM((lines, channels), BF16),
            pltpu.VMEM((sequences, cols), jnp.int32),
            pltpu.VMEM((narrow, channels), BF16),
            pltpu.VMEM((narrow, channels), BF16),
            pltpu.VMEM((turns, sequences, right_lanes), BF16),
            pltpu.SemaphoreType.DMA,
            pltpu.SemaphoreType.DMA,
            pltpu.SemaphoreType.DMA,
            pltpu.SemaphoreType.DMA,
            pltpu.SemaphoreType.DMA((row_count,)),
        ],
        [hbm] * 4,
        (hbm, VMEM),
    )(*in_hbm([alignment.reshape(lines, channels), alignment_mask, outer_product_left.T, outer_product_right.T]))
    right = lax.all_to_all(right, "row", split_axis=0, concat_axis=0, tiled=True)
    right = right.reshape(row_count * sequences, right_lanes)
    places_of = [(row, col) for row in range(row_count) for col in range(col_count)]

    def route(to):
        return [(row * col_count + col, to(row, col)[0] * col_count + to(row, col)[1]) for row, col in places_of]

    def near(d, k):
        return route(lambda row, col: (row // turns * turns + (row + d) % turns, partner(col, k, col_count)))

    def exchange(values):
        given = []
        for d in range(1, turns):
            part = lax.dynamic_slice_in_dim(values, (x + d) % turns * rows, rows, 1)
            given.append(lax.ppermute(part, ("row", "col"), near(d, 0)))
        return given

    turned = route(lambda row, col: (turns * col + row % turns, turned_column(row // turns, col_count)))
    left = lax.ppermute(left, ("row", "col"), turned)
    across = [left] + [lax.ppermute(left, ("row", "col"), near(d, 0)) for d in range(1, turns)]
    blocks = {(d, 0): value for d, value in enumerate(across)}
    if col_count & (col_count - 1) == 0:
        bit = col_count // 2
        while bit:
            for d, k in list(blocks):
                blocks[d, k | bit] = lax.ppermute(blocks[d, k], ("row", "col"), near(0, bit))
            bit //= 2
    else:
        for d in range(turns):
            for k in range(1, col_count):
                blocks[d, k] = lax.ppermute(across[d], ("row", "col"), near(0, k))
    lefts = [blocks[d, k] for d in range(turns) for k in range(col_count)]
    pairs = exchange(pair_features)

    block, tri_rows, pair_mask = call(
        functools.partial(prepare_kernel, own),
        16,
        [((places, width), BF16), ((4 * inner, width), BF16), ((1, places), F32)],
        [],
    )(residue_mask.reshape(1, -1), triangle_proj, pair_features, *pairs)

    first, gated = call(
        functools.partial(outer_kernel, cols, rows, narrow, turns),
        24,
        [((places, width), BF16), ((owners, 2 * own, places), BF16)],
        [
            pltpu.VMEM((row_count * sequences, left_lanes), BF16),
            pltpu.VMEM((row_count * sequences // LANES, rows * narrow, LANES), F32),
            pltpu.VMEM((narrow * narrow, width), F32),
            pltpu.VMEM((pieces, cols // members * rows * 2, narrow // pieces * LANES // 2), BF16),
            pltpu.VMEM((2, narrow // pieces * LANES // 2, members // 2 * width), BF16),
            pltpu.VMEM((places, width), F32),
            pltpu.VMEM((places, width), F32),
        ],
    )(right, block, outer_proj, tri_rows, pair_mask, *lefts)

    first = first.reshape(rows, cols, width)
    firsts = exchange(first)
    first_t, gate = call(gate_kernel, 16, [((width, places), F32)] * 2, [pltpu.VMEM((places, width), F32)])(
        first, triangle_gate, *firsts
    )
    triangle = triangle_by_channel if by_channel else triangle_by_residue
    summed = triangle(row_count, col_count, rows, cols, gated)
    (out,) = call(tail_kernel, 16, [((places, width), BF16)], [pltpu.VMEM((inner, places), F32)])(
        first_t, gate, summed, triangle_out, transition_in, transition_out
    )
    return out.reshape(rows, cols, width)


def solution(mesh):
    placed = (
        P("row", "col", None),
        P("row", "col"),
        P(),
        P("row", "col", None),
    ) + (P(),) * 8

    def body(*args):
        return shards(mesh.shape["row"], mesh.shape["col"], *args)

    return jax.shard_map(body, mesh=mesh, in_specs=placed, out_specs=P("row", "col", None), check_vma=False)
```

```python
import functools

import jax
import jax.numpy as jnp
from jax import lax
from jax.experimental import pallas as pl
from jax.experimental.pallas import tpu as pltpu
from jax.sharding import PartitionSpec as P


epsilon = 1e-05
LANES = 128
ABSENT = 2.0**100
BF16 = jnp.bfloat16
F32 = jnp.float32
NT = (((1,), (1,)), ((), ()))
TN = (((0,), (0,)), ((), ()))


def matmul(a, b, dims=(((1,), (0,)), ((), ()))):
    return lax.dot_general(a, b, dims, preferred_element_type=F32)


def iota(shape, axis):
    return lax.broadcasted_iota(jnp.int32, shape, axis)


def normalize(values, axis=-1):
    mean_value = jnp.mean(values, axis=axis, keepdims=True)
    centered = values - mean_value
    variance = jnp.mean(centered * centered, axis=axis, keepdims=True)
    return centered * lax.rsqrt(variance + epsilon)


def in_hbm(values):
    return [pltpu.with_memory_space_constraint(value, pltpu.HBM) for value in values]


def call(kernel, mebibytes, outs, scratch, in_specs=None, out_specs=None):
    return pl.pallas_call(
        kernel,
        out_shape=tuple(jax.ShapeDtypeStruct(*out) for out in outs),
        out_specs=out_specs or (VMEM,) * len(outs),
        scratch_shapes=scratch,
        compiler_params=pltpu.CompilerParams(vmem_limit_bytes=mebibytes * 1024 * 1024),
        **({} if in_specs is None else {"in_specs": in_specs}),
    )


VMEM = pl.BlockSpec(memory_space=pltpu.VMEM)


def pack_side(projected, mask, narrow, first, count, put, marked=False):
    sequences, cols = mask.shape
    members = LANES // narrow
    lane = iota((sequences, LANES), 1)
    groups = count // members
    width = groups * LANES
    residue = first + iota((cols, width), 1) // narrow
    masks = matmul(mask, (iota((cols, width), 0) == residue).astype(BF16))
    for group in range(groups):
        value = None
        for member in range(members):
            part = projected[pl.ds(first + group * members + member, sequences, stride=cols), :]
            value = part if value is None else jnp.where(lane >= member * narrow, part, value)
        kept = masks[:, group * LANES : (group + 1) * LANES]
        put(group, (jnp.where(kept > 0.5, value, ABSENT) if marked else value * kept).astype(BF16))
    if marked:
        return
    at = iota((cols, LANES), 1)
    pick = (iota((cols, LANES), 0) - first == at) & (at < count)
    put(groups, matmul(mask, pick.astype(BF16)).astype(BF16))


def side_kernel(
    narrow, align_hbm, mask_hbm, left_w_hbm, right_w_hbm, right_ref, left_ref,
    left_rows, right_rows, align, mask_int, left_w, right_w, align_sem, mask_sem, left_sem, right_sem,
):
    fetches = [
        pltpu.make_async_copy(left_w_hbm, left_w, left_sem),
        pltpu.make_async_copy(right_w_hbm, right_w, right_sem),
        pltpu.make_async_copy(align_hbm, align, align_sem),
        pltpu.make_async_copy(mask_hbm, mask_int, mask_sem),
    ]
    for copy in fetches:
        copy.start()
    for copy in fetches:
        copy.wait()
    members = LANES // narrow
    both = jnp.concatenate([left_w[...]] * members + [right_w[...]] * members, axis=0)
    normed = normalize(align[...].astype(F32)).astype(BF16)
    value = matmul(normed, both, NT)
    left_rows[...] = value[:, :LANES]
    right_rows[...] = value[:, LANES:]
    mask = mask_int[...].astype(BF16)
    cols = mask.shape[1]
    copies = right_ref.shape[0]
    parts = cols * narrow // right_ref.shape[2]
    for h in range(parts):

        def put_right(group, value):
            for n in range(h, copies, parts):
                right_ref[n, :, group * LANES : (group + 1) * LANES] = value

        pack_side(right_rows, mask, narrow, h * (cols // parts), cols // parts, put_right, True)

    def put_left(group, value):
        left_ref[:, group * LANES : (group + 1) * LANES] = value

    pack_side(left_rows, mask, narrow, 0, cols, put_left)


def prepare_kernel(own, residue_ref, tri_ref, pair_ref, *refs):
    *given_refs, block_ref, tri_rows_ref, pair_mask_ref = refs
    rows, cols, _ = pair_ref.shape
    parts = cols // rows
    row = lax.axis_index("row")
    x = lax.rem(row, parts)
    present = residue_ref[...].astype(BF16)
    residue = iota((present.shape[1], 1), 0)
    place = iota((1, pair_mask_ref.shape[1]), 1)
    tall = lax.div(row, parts) * cols + place % cols
    short = lax.axis_index("col") * cols + x * rows + place // cols
    pair_mask_ref[...] = matmul(present, (residue == tall).astype(BF16)) * matmul(
        present, (residue == short).astype(BF16)
    )
    for i in range(rows):
        at = pl.ds(pl.multiple_of((x * rows + i) * rows, 8), rows)
        block_ref[at, :] = pair_ref[i, pl.ds(pl.multiple_of(x * rows, 8), rows), :]
        for d, given_ref in enumerate(given_refs, 1):
            at = pl.ds(pl.multiple_of((lax.rem(x - d + parts, parts) * rows + i) * rows, 8), rows)
            block_ref[at, :] = given_ref[i]
    out = tri_ref.shape[0]
    at = iota((4 * out, 4 * out), 0)
    kind, rest = at // (2 * out), at % (2 * out)
    owner, side, channel = rest // (2 * own), rest // own % 2, rest % own
    column = side * 2 * out + kind * out + owner * own + channel
    pick = (iota((4 * out, 4 * out), 1) == column).astype(BF16)
    tri_rows_ref[...] = matmul(pick, tri_ref[...], NT).astype(BF16)


def outer_kernel(tall, short, narrow, parts, right_ref, pair_ref, proj_ref, tri_ref, pair_mask_ref, *refs):
    *left_refs, first_ref, tri_out_ref, left, right_t, proj, stacked, spread, moved, rounded = refs
    sources = len(left_refs) // parts
    sequences = left_refs[0].shape[0]
    x, column = lax.rem(lax.axis_index("row"), parts), lax.axis_index("col")
    for n, left_ref in enumerate(left_refs):
        d, k = n // sources, n % sources
        plane = turned_column(source(column, k, sources), sources)
        start = (plane * parts + lax.rem(x - d + parts, parts)) * sequences
        left[pl.ds(pl.multiple_of(start, sequences), sequences), :] = left_ref[...]
    members = LANES // narrow
    groups = tall // members
    left_width = tall * narrow
    width = pair_ref.shape[1]
    planes = right_t.shape[0]
    for p in range(planes):
        right_t[p] = right_ref[p * LANES : (p + 1) * LANES, :].astype(F32).T
    proj[...] = proj_ref[...].astype(F32)
    steps = stacked.shape[0]
    step = narrow // steps
    spread[...] = jnp.zeros_like(spread)
    total = None
    for n in range(steps):
        some = []
        for p in range(planes):
            each = [right_t.at[p][pl.ds(n * step + d, short, stride=narrow), :] for d in range(step)]
            each = jnp.concatenate(each, axis=0)
            some.append(jnp.where(each < ABSENT / 2, each, 0.0).astype(BF16))
        block = matmul(jnp.concatenate(some, axis=1), left[:, :left_width])
        for e in range(0, step, 2):
            lanes = slice(e // 2 * LANES, (e // 2 + 1) * LANES)
            for g in range(0, groups, 2):
                pairs = []
                for d in (e, e + 1):
                    two = [
                        block[d * short : (d + 1) * short, (g + m) * LANES : (g + m + 1) * LANES] for m in range(2)
                    ]
                    pairs.append(jnp.concatenate(two, axis=0).astype(BF16))
                for side in range(2):
                    half = slice(side * LANES // 2, (side + 1) * LANES // 2)
                    at = side * groups * short + g * short
                    stacked[n, at : at + 2 * short, lanes] = jnp.concatenate([v[:, half] for v in pairs], axis=1)
        for d in range(step):
            part = proj[pl.ds(n * step + d, narrow, stride=narrow), :].astype(BF16)
            for m in range(members // 2):
                start = d * LANES // 2 + m * narrow
                spread[n % 2, start : start + narrow, m * width : (m + 1) * width] = part
        term = matmul(stacked[n], spread[n % 2])
        total = term if total is None else total + term
    present = [right_t.at[p][pl.ds(0, short, stride=narrow), :] < ABSENT / 2 for p in range(planes)]
    counts = matmul(jnp.concatenate(present, axis=1).astype(BF16), left[:, left_width:])
    scale = 1.0 / jnp.maximum(counts, 1.0)
    for g in range(groups):
        for m in range(members):
            i = g * members + m
            at = slice(i * short, (i + 1) * short)
            side, n = m // (members // 2), m % (members // 2)
            start = (side * groups + g) * short
            part = total[start : start + short, n * width : (n + 1) * width]
            moved[at, :] = part * scale[:, i : i + 1] + pair_ref[at, :].astype(F32)
    for j in range(short):
        first = moved[pl.ds(j, tall, stride=short), :].astype(BF16)
        first_ref[j * tall : (j + 1) * tall, :] = first
        rounded[j * tall : (j + 1) * tall, :] = first.astype(F32)
    devices, pair, _ = tri_out_ref.shape
    half = devices * pair
    projections = matmul(tri_ref[...], normalize(rounded[...].T, 0).astype(BF16))
    gated = jax.nn.sigmoid(projections[:half]) * projections[half:] * pair_mask_ref[...]
    gated = gated.astype(BF16)
    for d in range(devices):
        tri_out_ref[d] = gated[d * pair : (d + 1) * pair, :]


def triangle_kernel(row_count, col_count, rows, cols, own, given_ref, out_ref, opened, summed):
    pair = 2 * own
    planes = opened.shape[0]
    parts = cols // rows
    each = -(-col_count // planes)
    used = each * cols

    def open_column(c, carry):
        for a in range(col_count):
            lanes = slice(a % each * cols, (a % each + 1) * cols)
            for x in range(parts):
                value = given_ref[(a * parts + x) * col_count + c].astype(F32)
                for k in range(rows):
                    start = pl.multiple_of((c * cols + x * rows + k) * pair, pair)
                    opened[a // each, pl.ds(start, pair), lanes] = value[:, k * cols : (k + 1) * cols]
        return carry

    residues = row_count * rows
    folds = 2 if planes == 2 and residues == 2 * used else 1
    lax.fori_loop(0, col_count, open_column, 0)
    for t in range(own):
        left = [opened.at[p][pl.ds(t, residues, stride=pair), :].astype(BF16) for p in range(planes)]
        right = [opened.at[p][pl.ds(own + t, residues, stride=pair), :].astype(BF16) for p in range(planes)]
        for p in range(planes):
            count = min(used, residues - p * used)
            for q in range(planes):
                total = matmul(left[p], right[q], TN)[:count]
                start = p * own if folds == 2 else p * used * pair
                summed.at[q][pl.ds(start + t, count, stride=pair), :] = total

    def close_row(r, carry):
        for c in range(col_count):
            lanes = slice(c % each * cols, (c % each + 1) * cols)
            parts = []
            for i in range(rows):
                start = pl.multiple_of((r * rows + i) * pair, pair)
                parts.append(summed[c // each, pl.ds(start, pair), lanes])
            value = jnp.concatenate(parts, axis=1)
            for fold in range(folds):
                at = (r + fold * (row_count // folds)) * col_count + c
                out_ref[at] = value[fold * own : (fold + 1) * own].astype(BF16)
        return carry

    lax.fori_loop(0, row_count // folds, close_row, 0)


def partner(index, k, count):
    return index ^ k if count & (count - 1) == 0 else (index + k) % count


def turned_column(plane, count):
    return plane ^ (count // 2) if count & (count - 1) == 0 else plane


def source(index, k, count):
    return index ^ k if count & (count - 1) == 0 else lax.rem(index - k + count, count)


def triangle_by_channel(row_count, col_count, rows, cols, gated):
    devices, pair, places = gated.shape
    own = pair // 2
    gated = lax.all_to_all(gated, ("row", "col"), split_axis=0, concat_axis=0, tiled=True)
    residues = row_count * rows
    planes = -(-col_count // (LANES // cols))
    (summed,) = call(
        functools.partial(triangle_kernel, row_count, col_count, rows, cols, own),
        16,
        [((devices, own, places), BF16)],
        [pltpu.VMEM((planes, residues * pair, LANES), F32)] * 2,
    )(gated)
    summed = lax.all_to_all(summed, ("row", "col"), split_axis=0, concat_axis=0, tiled=True)
    return summed


def triangle_by_residue(row_count, col_count, rows, cols, gated):
    _, pair, places = gated.shape
    both = gated.reshape(2, pair // 2, cols, rows).transpose(0, 3, 2, 1)
    right = lax.all_gather(both[1], "row", axis=0, tiled=True)
    right = lax.all_to_all(right, "col", split_axis=0, concat_axis=1, tiled=True)
    left = lax.all_gather(both[0], "col", axis=1, tiled=True)
    summed = jnp.einsum("ikc,jkc->cij", left, right, preferred_element_type=F32)
    return summed.reshape(1, pair // 2, places).astype(BF16)


def gate_kernel(first_ref, gate_w_ref, *refs):
    *given_refs, first_t_ref, gated_ref, home = refs
    rows, cols, _ = first_ref.shape
    parts = cols // rows
    x = lax.rem(lax.axis_index("row"), parts)
    for j in range(rows):
        value = first_ref[j, pl.ds(pl.multiple_of(x * rows, 8), rows), :]
        home[pl.ds(x * rows + j, rows, stride=cols), :] = value.astype(F32)
        for d, given_ref in enumerate(given_refs, 1):
            at = pl.ds(lax.rem(x - d + parts, parts) * rows + j, rows, stride=cols)
            home[at, :] = given_ref[j].astype(F32)
    first_t = home[...].T
    first_t_ref[...] = first_t
    gated_ref[...] = jax.nn.sigmoid(matmul(gate_w_ref[...].T, normalize(first_t, 0).astype(BF16)))


def tail_kernel(first_ref, gated_ref, summed_ref, out_w_ref, in_ref, back_ref, out_ref, summed):
    own = summed_ref.shape[1]
    for d in range(summed_ref.shape[0]):
        summed[d * own : (d + 1) * own, :] = summed_ref[d].astype(F32)
    normed_sum = normalize(summed[...], 0).astype(BF16)
    update = gated_ref[...] * matmul(out_w_ref[...].T, normed_sum)
    second = (first_ref[...] + update).astype(BF16).astype(F32)
    normed_second = normalize(second, 0).astype(BF16)
    hidden = jnp.maximum(matmul(in_ref[...].T, normed_second), 0.0).astype(BF16)
    result = second + matmul(back_ref[...].T, hidden)
    out_ref[...] = result.T.astype(BF16)


def shards(
    row_count, col_count, alignment, alignment_mask, residue_mask, pair_features, outer_product_left, outer_product_right,
    outer_proj, triangle_proj, triangle_gate, triangle_out, transition_in, transition_out,
):
    rows, cols, width = pair_features.shape
    sequences, _, channels = alignment.shape
    narrow = outer_product_left.shape[1]
    inner = triangle_out.shape[0]
    devices = row_count * col_count
    turns = cols // rows
    places = rows * cols
    r = lax.axis_index("row")
    by_channel = inner % devices == 0
    owners = devices if by_channel else 1
    own = inner // owners
    members = LANES // narrow
    right_lanes = rows * narrow
    left_lanes = cols * narrow + LANES
    lines = sequences * cols
    pieces = 8 if narrow % 16 == 0 else 1
    x = r % turns

    hbm = pl.BlockSpec(memory_space=pltpu.HBM)
    right, left = call(
        functools.partial(side_kernel, narrow),
        16,
        [((row_count, sequences, right_lanes), BF16), ((sequences, left_lanes), BF16)],
        [
            pltpu.VMEM((lines, LANES), F32),
            pltpu.VMEM((lines, LANES), F32),
            pltpu.VMEM((lines, channels), BF16),
            pltpu.VMEM((sequences, cols), jnp.int32),
            pltpu.VMEM((narrow, channels), BF16),
            pltpu.VMEM((narrow, channels), BF16),
            pltpu.SemaphoreType.DMA,
            pltpu.SemaphoreType.DMA,
            pltpu.SemaphoreType.DMA,
            pltpu.SemaphoreType.DMA,
        ],
        [hbm] * 4,
    )(*in_hbm([alignment.reshape(lines, channels), alignment_mask, outer_product_left.T, outer_product_right.T]))
    right = lax.all_to_all(right, "row", split_axis=0, concat_axis=0, tiled=True)
    right = right.reshape(row_count * sequences, right_lanes)
    places_of = [(row, col) for row in range(row_count) for col in range(col_count)]

    def route(to):
        return [(row * col_count + col, to(row, col)[0] * col_count + to(row, col)[1]) for row, col in places_of]

    def near(d, k):
        return route(lambda row, col: (row // turns * turns + (row + d) % turns, partner(col, k, col_count)))

    def exchange(values):
        given = []
        for d in range(1, turns):
            part = lax.dynamic_slice_in_dim(values, (x + d) % turns * rows, rows, 1)
            given.append(lax.ppermute(part, ("row", "col"), near(d, 0)))
        return given

    turned = route(lambda row, col: (turns * col + row % turns, turned_column(row // turns, col_count)))
    left = lax.ppermute(left, ("row", "col"), turned)
    across = [left] + [lax.ppermute(left, ("row", "col"), near(d, 0)) for d in range(1, turns)]
    blocks = {(d, 0): value for d, value in enumerate(across)}
    if col_count & (col_count - 1) == 0:
        bit = col_count // 2
        while bit:
            for d, k in list(blocks):
                blocks[d, k | bit] = lax.ppermute(blocks[d, k], ("row", "col"), near(0, bit))
            bit //= 2
    else:
        for d in range(turns):
            for k in range(1, col_count):
                blocks[d, k] = lax.ppermute(across[d], ("row", "col"), near(0, k))
    lefts = [blocks[d, k] for d in range(turns) for k in range(col_count)]
    pairs = exchange(pair_features)

    block, tri_rows, pair_mask = call(
        functools.partial(prepare_kernel, own),
        16,
        [((places, width), BF16), ((4 * inner, width), BF16), ((1, places), F32)],
        [],
    )(residue_mask.reshape(1, -1), triangle_proj, pair_features, *pairs)

    first, gated = call(
        functools.partial(outer_kernel, cols, rows, narrow, turns),
        24,
        [((places, width), BF16), ((owners, 2 * own, places), BF16)],
        [
            pltpu.VMEM((row_count * sequences, left_lanes), BF16),
            pltpu.VMEM((row_count * sequences // LANES, rows * narrow, LANES), F32),
            pltpu.VMEM((narrow * narrow, width), F32),
            pltpu.VMEM((pieces, cols // members * rows * 2, narrow // pieces * LANES // 2), BF16),
            pltpu.VMEM((2, narrow // pieces * LANES // 2, members // 2 * width), BF16),
            pltpu.VMEM((places, width), F32),
            pltpu.VMEM((places, width), F32),
        ],
    )(right, block, outer_proj, tri_rows, pair_mask, *lefts)

    first = first.reshape(rows, cols, width)
    firsts = exchange(first)
    first_t, gate = call(gate_kernel, 16, [((width, places), F32)] * 2, [pltpu.VMEM((places, width), F32)])(
        first, triangle_gate, *firsts
    )
    triangle = triangle_by_channel if by_channel else triangle_by_residue
    summed = triangle(row_count, col_count, rows, cols, gated)
    (out,) = call(tail_kernel, 16, [((places, width), BF16)], [pltpu.VMEM((inner, places), F32)])(
        first_t, gate, summed, triangle_out, transition_in, transition_out
    )
    return out.reshape(rows, cols, width)


def solution(mesh):
    placed = (
        P("row", "col", None),
        P("row", "col"),
        P(),
        P("row", "col", None),
    ) + (P(),) * 8

    def body(*args):
        return shards(mesh.shape["row"], mesh.shape["col"], *args)

    return jax.shard_map(body, mesh=mesh, in_specs=placed, out_specs=P("row", "col", None), check_vma=False)
```
